32 devices in a mesh: pb: 4 (over y, core), ka: 8 (over z, x).
Axes of the slice: x: 2, y: 2, z: 4, core: 2. Of those that a mesh axis runs over, the one named last changes fastest.
Arguments:
- queries: float32 [2048, 128], P('pb'), may hold values from -36 to 36
- cache_keys: float32 [65536, 128], P('ka'), may hold values from -4 to 4
- cache_values: float32 [65536, 128], P('ka'), may hold values from -6 to 6
- kept_index: int32 [4096], P('ka'), may hold values from 0 to 65535, as said below
Outputs:
- fitted: float32 [4096, 128], P('ka')
The draws below stay inside these ranges and needn't reach their ends.
Inputs may be any that keep to these rules, and one draw needn't show every extreme that they name: `kept_index`: Increasing; the t-th kept index lies among the cache rows t * (16) to (t + 1) * 16 - 1, so the kept keys of a device are rows of its own block of the cache.
All inputs are finite; a program needn't handle non-finite values.
Results may differ from the reference program's by a relative error of at most 0.0003.
Values sent between devices are 32-bit elements; how exact they have to be, the bound alone decides.
A program may use at most 128 MiB of HBM per device.

```python
import math
import jax
import jax.numpy as jnp
from jax import lax

HEAD = 128
KEEP_DEV = 512
CACHE_DEV = 8192
ITERS = 2
NQ = 2048
KEEP = 4096
CACHE = 65536


def kept_rows(key):
    stride = CACHE_DEV // KEEP_DEV
    offsets = jax.random.randint(jax.random.fold_in(key, 11), (KEEP,), 0, stride).astype(jnp.int32)
    offsets = offsets.at[0].set(0).at[KEEP - 1].set(stride - 1)
    positions = jnp.arange(KEEP, dtype=jnp.int32)
    return positions * stride + offsets


def draw_kept_index(key, part):
    return kept_rows(key).astype(jnp.int32)


def draw_cache_keys(key, part):
    drawn = jax.random.normal(jax.random.fold_in(key, 21), (CACHE, HEAD), jnp.float32)
    return jnp.clip(drawn, -4.0, 4.0)


def draw_queries(key, part):
    drawn = 3.0 * jax.random.normal(jax.random.fold_in(key, 31), (NQ, HEAD), jnp.float32)
    return jnp.clip(drawn, -36.0, 36.0)


def levels(key, dims, cuts, least, largest):
    factor_of, own = 1.0, jax.random.fold_in(key, 6)
    for dim, shards_of in cuts:
        heights = jnp.exp(jax.random.uniform(jax.random.fold_in(own, dim), (shards_of,), jnp.float32, least / len(cuts), largest / len(cuts)))
        factor_of = factor_of * jnp.repeat(heights, dims[dim] // shards_of).reshape([-1 if axis == dim else 1 for axis in range(len(dims))])
    return factor_of


def noise(rng, shape, deviation, limit, cuts=(), kind=jnp.bfloat16):
    result = jax.random.normal(rng, shape, jnp.float32) * deviation
    if len(cuts) > 0:
        result = levels(rng, shape, cuts, -0.22, 0.18) * result
    return jnp.clip(result, min=-limit, max=limit).astype(kind)


def setup_inputs(seed: int = 0) -> dict:
    splits = jax.random.split(jax.random.key(seed), 5)
    return {
        "queries": draw_queries(jax.random.fold_in(splits[4], 71), 0),
        "cache_keys": draw_cache_keys(jax.random.fold_in(splits[4], 71), 0),
        "cache_values": noise(splits[2], (CACHE, HEAD), 1.0, 6.0, ((0, 8),), jnp.float32),
        "kept_index": draw_kept_index(jax.random.fold_in(splits[4], 71), 0),
    }


ridge_weight = 0.01
highest = lax.Precision.HIGHEST

def softmax_rows(scores):
    top_row = lax.optimization_barrier(jnp.max(scores, axis=1, keepdims=True))
    exponent_rows = jnp.exp(scores - top_row)
    return exponent_rows / lax.optimization_barrier(jnp.sum(exponent_rows, axis=1, keepdims=True))

def reference(queries, cache_keys, cache_values, kept_index):
    inverse_root = 1.0 / math.sqrt(HEAD)
    block_rows = min(512, NQ)
    query_blocks = queries.reshape(NQ // block_rows, block_rows, HEAD)
    kept_keys = jnp.take(cache_keys, kept_index.astype(jnp.int32), axis=0)

    def target_block(query_rows):
        scores = jnp.dot(query_rows, cache_keys.T, precision=highest) * inverse_root
        return jnp.dot(softmax_rows(scores), cache_values, precision=highest)
    target = lax.map(target_block, query_blocks)

    def weights_of(query_rows):
        scores = jnp.dot(query_rows, kept_keys.T, precision=highest) * inverse_root
        return softmax_rows(scores)

    def project_back(rows_in):

        def add_block(running, block_pair):
            query_rows, side_rows = block_pair
            return (running + jnp.dot(weights_of(query_rows).T, side_rows, precision=highest), None)
        running, unused = lax.scan(add_block, jnp.zeros((KEEP, HEAD), jnp.float32), (query_blocks, rows_in))
        return running

    def forward(direction):
        return lax.map(lambda query_rows: jnp.dot(weights_of(query_rows), direction, precision=highest), query_blocks)
    residual = project_back(target)
    fitted = jnp.zeros((KEEP, HEAD), jnp.float32)
    direction = residual
    norm_now = lax.optimization_barrier(jnp.sum(residual * residual, axis=0))
    for iteration in range(ITERS):
        updates = forward(direction)
        operator_image = project_back(updates) + ridge_weight * direction
        step_length = norm_now / lax.optimization_barrier(jnp.sum(direction * operator_image, axis=0))
        fitted = fitted + step_length * direction
        if iteration + 1 < ITERS:
            residual = residual - step_length * operator_image
            norm_next = lax.optimization_barrier(jnp.sum(residual * residual, axis=0))
            direction = residual + norm_next / norm_now * direction
            norm_now = norm_next
    return fitted
```

```python
import functools
import math

import jax
import jax.numpy as jnp
from jax import lax
from jax.experimental import pallas as pl
from jax.experimental.pallas import tpu as pltpu
from jax.sharding import PartitionSpec as P

ITERS = 2


ridge_weight = 0.01
highest = lax.Precision.HIGHEST


def contract(left_side, right_side, left_dim, right_dim):
    return lax.dot_general(
        left_side,
        right_side,
        (((left_dim,), (right_dim,)), ((), ())),
        precision=highest,
        preferred_element_type=jnp.float32,
    )


def column_sums(left_side, right_side):
    return jnp.sum(left_side * right_side, axis=0, keepdims=True)


def fit_kernel(
    ka_size,
    pb_size,
    part_ref,
    kept_ref,
    fitted_ref,
    flipped,
    stats_in,
    stats_all,
    ka_out,
    ka_in,
    ka_all,
    pb_out,
    pb_in,
    pb_all,
    tail_out,
    tail_in,
    ka_send,
    ka_recv,
    pb_send,
    pb_recv,
):
    ka_me = lax.axis_index("ka")
    pb_me = lax.axis_index("pb")
    width = fitted_ref.shape[1]
    query_rows = kept_ref.shape[0]
    kept_rows = kept_ref.shape[1]
    ka_share = query_rows // ka_size
    pb_share = kept_rows // pb_size

    def peer_of(axis, offset):
        size = ka_size if axis == "ka" else pb_size
        me = ka_me if axis == "ka" else pb_me
        return lax.rem(me + offset, size)

    barrier = pltpu.get_barrier_semaphore()
    for axis, size in (("ka", ka_size), ("pb", pb_size)):
        for offset in range(1, size):
            pl.semaphore_signal(
                barrier,
                inc=1,
                device_id={axis: peer_of(axis, offset)},
                device_id_type=pl.DeviceIdType.MESH,
            )
    pl.semaphore_wait(barrier, ka_size + pb_size - 2)

    def begin(axis, phase, source_of, target):
        size, send, recv = (
            (ka_size, ka_send, ka_recv) if axis == "ka" else (pb_size, pb_send, pb_recv)
        )
        copies = []
        for offset in range(1, size):
            peer = peer_of(axis, offset)
            copy = pltpu.make_async_remote_copy(
                src_ref=source_of(peer),
                dst_ref=target,
                send_sem=send.at[phase, offset],
                recv_sem=recv.at[phase, offset],
                device_id={axis: peer},
                device_id_type=pl.DeviceIdType.MESH,
            )
            copy.start()
            copies.append(copy)
        return copies

    def finish(copies):
        for copy in copies:
            copy.wait()

    def scattered_sum(axis, phase, value, tail, out, arrived, whole):
        me, size, share = (
            (ka_me, ka_size, ka_share) if axis == "ka" else (pb_me, pb_size, pb_share)
        )
        out[:, :share, :] = value.reshape(size, share, width)
        out[:, share:, :] = jnp.broadcast_to(tail[None], (size, 8, width))
        copies = begin(axis, phase, lambda peer: out.at[peer], arrived.at[me])
        arrived[me] = out[me]
        finish(copies)
        total = arrived[0]
        for source in range(1, size):
            total = total + arrived[source]
        whole[me] = total[:share]
        finish(begin(axis, phase + 1, lambda peer: whole.at[me], whole.at[me]))
        return whole[...].reshape(size * share, width), total[share:]

    def matmul(left_side, right_side):
        return jnp.dot(
            left_side, right_side, precision=highest, preferred_element_type=jnp.float32
        )

    def tail_rows(*rows):
        place = lax.broadcasted_iota(jnp.int32, (8, width), 0)
        tail = jnp.zeros((8, width), jnp.float32)
        for number, row in enumerate(rows):
            tail = jnp.where(place == number, row, tail)
        return tail

    copies = begin("ka", 0, lambda peer: part_ref.at[peer], stats_in.at[ka_me])
    stats_in[ka_me] = part_ref[ka_me]
    flipped[...] = kept_ref[...].T
    finish(copies)

    def column(source, number):
        return stats_in[source, :, width + number : width + number + 1]

    top = column(0, 0)
    kept_top = column(0, 2)
    for source in range(1, ka_size):
        top = jnp.maximum(top, column(source, 0))
        kept_top = jnp.maximum(kept_top, column(source, 2))
    total = jnp.zeros_like(top)
    kept_total = jnp.zeros_like(top)
    numerator = jnp.zeros((ka_share, width), jnp.float32)
    for source in range(ka_size):
        factor = jnp.exp(column(source, 0) - top)
        total = total + column(source, 1) * factor
        numerator = numerator + stats_in[source, :, :width] * factor
        kept_total = kept_total + column(source, 3) * jnp.exp(column(source, 2) - kept_top)
    lane = lax.broadcasted_iota(jnp.int32, (ka_share, width), 1)
    stats_all[ka_me, :, :width] = numerator / total
    stats_all[ka_me, :, width:] = jnp.where(lane == 0, kept_top, kept_total)
    finish(begin("ka", 1, lambda peer: stats_all.at[ka_me], stats_all.at[ka_me]))
    target = stats_all[:, :, :width].reshape(query_rows, width)
    joint_top = stats_all[:, :, width : width + 1].reshape(query_rows, 1)
    joint_total = stats_all[:, :, width + 1 : width + 2].reshape(query_rows, 1)
    own_top = part_ref[:, :, width + 2 : width + 3].reshape(query_rows, 1)
    scale = jnp.exp(own_top - joint_top) / joint_total

    no_tail = jnp.zeros((8, width), jnp.float32)
    residual, _ = scattered_sum(
        "pb",
        0,
        matmul(flipped[...], scale * target),
        no_tail,
        pb_out.at[0],
        pb_in.at[0],
        pb_all.at[0],
    )
    fitted = jnp.zeros_like(residual)
    direction = residual
    updates = None
    norm_now = None
    length_now = None
    for iteration in range(ITERS):
        forward = scale * matmul(kept_ref[...], residual)
        tail = tail_rows(column_sums(residual, residual), column_sums(residual, direction))
        summed, tail = scattered_sum(
            "ka",
            2 + 2 * iteration,
            forward,
            tail,
            ka_out.at[iteration],
            ka_in.at[iteration],
            ka_all.at[iteration],
        )
        norm_next = tail[0:1]
        if iteration == 0:
            updates = summed
            length_now = norm_next
        else:
            ratio = norm_next / norm_now
            direction = residual + ratio * direction
            updates = summed + ratio * updates
            length_now = norm_next + 2.0 * ratio * tail[1:2] + ratio * ratio * length_now
        norm_now = norm_next
        energy = tail_rows(column_sums(updates, updates))
        if iteration + 1 == ITERS:
            tail_out[...] = energy
            copies = begin("pb", 2 * ITERS, lambda peer: tail_out, tail_in.at[pb_me])
            tail_in[pb_me] = energy
            finish(copies)
            energy = tail_in[0]
            for source in range(1, pb_size):
                energy = energy + tail_in[source]
            step_length = norm_now / (energy[0:1] + ridge_weight * length_now)
            fitted_ref[...] = fitted + step_length * direction
        else:
            image, energy = scattered_sum(
                "pb",
                2 + 2 * iteration,
                matmul(flipped[...], scale * updates),
                energy,
                pb_out.at[iteration + 1],
                pb_in.at[iteration + 1],
                pb_all.at[iteration + 1],
            )
            step_length = norm_now / (energy[0:1] + ridge_weight * length_now)
            fitted = fitted + step_length * direction
            residual = residual - step_length * (image + ridge_weight * direction)


def fit(part, kept_exponent):
    ka_size, pb_size = lax.axis_size("ka"), lax.axis_size("pb")
    query_rows, kept_rows = kept_exponent.shape
    width = part.shape[1] // 2
    ka_share, pb_share = query_rows // ka_size, kept_rows // pb_size
    space = functools.partial(pltpu.VMEM, dtype=jnp.float32)
    return pl.pallas_call(
        functools.partial(fit_kernel, ka_size, pb_size),
        out_shape=jax.ShapeDtypeStruct((kept_rows, width), jnp.float32),
        in_specs=[pl.BlockSpec(memory_space=pltpu.VMEM)] * 2,
        out_specs=pl.BlockSpec(memory_space=pltpu.VMEM),
        scratch_shapes=[
            space((kept_rows, query_rows)),
            space((ka_size, ka_share, 2 * width)),
            space((ka_size, ka_share, 2 * width)),
            space((ITERS, ka_size, ka_share + 8, width)),
            space((ITERS, ka_size, ka_share + 8, width)),
            space((ITERS, ka_size, ka_share, width)),
            space((ITERS, pb_size, pb_share + 8, width)),
            space((ITERS, pb_size, pb_share + 8, width)),
            space((ITERS, pb_size, pb_share, width)),
            space((8, width)),
            space((pb_size, 8, width)),
            pltpu.SemaphoreType.DMA((2 + 2 * ITERS, ka_size)),
            pltpu.SemaphoreType.DMA((2 + 2 * ITERS, ka_size)),
            pltpu.SemaphoreType.DMA((2 * ITERS + 1, pb_size)),
            pltpu.SemaphoreType.DMA((2 * ITERS + 1, pb_size)),
        ],
        compiler_params=pltpu.CompilerParams(
            collective_id=0, has_side_effects=True, vmem_limit_bytes=40 * 1024 * 1024
        ),
    )(part.reshape(ka_size, ka_share, 2 * width), kept_exponent)


def thirds(value):
    first = value.astype(jnp.bfloat16)
    rest = value - first.astype(jnp.float32)
    second = rest.astype(jnp.bfloat16)
    third = (rest - second.astype(jnp.float32)).astype(jnp.bfloat16)
    return first, second, third


def target_kernel(inverse_root, queries_ref, keys_ref, values_ref, kept_ref, part_ref, wide, top, total, sums):
    width = queries_ref.shape[1]

    @pl.when(pl.program_id(0) == 0)
    def _():
        one, two, three = thirds(queries_ref[...])
        wide[...] = jnp.concatenate((one, one, two, one, three, two), axis=1)
        top[...] = jnp.full_like(top, -jnp.inf)
        total[...] = jnp.zeros_like(total)
        sums[...] = jnp.zeros_like(sums)

    one, two, three = thirds(keys_ref[...])
    scores = (
        lax.dot_general(
            wide[...],
            jnp.concatenate((one, two, one, three, one, two), axis=1),
            (((1,), (1,)), ((), ())),
            preferred_element_type=jnp.float32,
        )
        * inverse_root
    )
    top_next = jnp.maximum(top[...], jnp.max(scores, axis=1, keepdims=True))
    factor = jnp.exp(top[...] - top_next)
    exponent = jnp.exp(scores - top_next)
    top[...] = top_next
    total[...] = total[...] * factor + jnp.sum(exponent, axis=1, keepdims=True)
    one, two, three = thirds(values_ref[...])
    high, middle, low = thirds(exponent)
    pair = jnp.concatenate((one, two), axis=1)
    product = functools.partial(jnp.dot, preferred_element_type=jnp.float32)
    both = product(high, pair) + product(middle, pair)
    small = product(high, three) + product(low, one)
    sums[...] = sums[...] * factor + (both[:, :width] + (both[:, width:] + small))

    @pl.when(pl.program_id(0) == pl.num_programs(0) - 1)
    def _():
        lane = lax.broadcasted_iota(jnp.int32, kept_ref.shape, 1)
        stats = jnp.where(lane == 0, top[...], jnp.where(lane == 1, total[...], kept_ref[...]))
        part_ref[:, :width] = sums[...]
        part_ref[:, width:] = stats


def target_part(queries, cache_keys, cache_values, kept_stats, inverse_root):
    query_rows, width = queries.shape
    block_size = min(2048, cache_keys.shape[0])
    fixed = pl.BlockSpec((query_rows, width), lambda block: (0, 0))
    moving = pl.BlockSpec((block_size, width), lambda block: (block, 0))
    return pl.pallas_call(
        functools.partial(target_kernel, inverse_root),
        grid=(cache_keys.shape[0] // block_size,),
        out_shape=jax.ShapeDtypeStruct((query_rows, 2 * width), jnp.float32),
        in_specs=[fixed, moving, moving, fixed],
        out_specs=pl.BlockSpec((query_rows, 2 * width), lambda block: (0, 0)),
        scratch_shapes=[
            pltpu.VMEM((query_rows, 6 * width), jnp.bfloat16),
            pltpu.VMEM((query_rows, 1), jnp.float32),
            pltpu.VMEM((query_rows, 1), jnp.float32),
            pltpu.VMEM((query_rows, width), jnp.float32),
        ],
        compiler_params=pltpu.CompilerParams(vmem_limit_bytes=40 * 1024 * 1024),
    )(queries, cache_keys, cache_values, kept_stats)


def halves(value):
    first = value.astype(jnp.bfloat16)
    return first, (value - first.astype(jnp.float32)).astype(jnp.bfloat16)


def product(left_side, right_side, left_dim=1, right_dim=0):
    return lax.dot_general(
        left_side,
        right_side,
        (((left_dim,), (right_dim,)), ((), ())),
        preferred_element_type=jnp.float32,
    )


def wide_queries(value):
    one, two, three = thirds(value)
    return jnp.concatenate((one, one, two, one, three, two), axis=1)


def wide_keys(value):
    one, two, three = thirds(value)
    return jnp.concatenate((one, two, one, three, one, two), axis=1)


def stacked(value):
    return jnp.concatenate(thirds(value), axis=0)


def folded(value):
    rows = value.shape[0] // 3
    return value[:rows] + (value[rows : 2 * rows] + value[2 * rows :])


def whole_kernel(
    ka_size,
    pb_size,
    exponent_scale,
    queries_ref,
    index_ref,
    keys_hbm,
    values_hbm,
    fitted_ref,
    keys_v,
    values_v,
    sums,
    queries_all,
    queries_wide,
    kept_all,
    part,
    part_in,
    stats,
    stats_in,
    first_part,
    second_part,
    kept_stats,
    scale,
    target_all,
    residual_v,
    half_out,
    core_in,
    side_out,
    side_in,
    updates_all,
    energy_out,
    energy_in,
    piece_out,
    piece_in,
    output_all,
    load_sems,
    ka_send,
    ka_recv,
    pb_send,
    pb_recv,
    pair_send,
    pair_recv,
):
    ka_me = lax.axis_index("ka")
    pb_me = lax.axis_index("pb")
    query_rows, width = queries_ref.shape
    columns = width // ka_size
    pieces = query_rows // 128
    group = kept_all.shape[1]
    cache_rows = keys_hbm.shape[0]
    block = cache_rows // pb_size
    stride = block // group
    half_width = 2 * query_rows
    core_bit = lax.rem(pb_me, 2)
    core_peer = pb_me + 1 - 2 * core_bit
    side_peer = lax.rem(pb_me + 2, 4)

    def peer_of(axis, offset):
        if axis == "ka":
            return lax.rem(ka_me + offset, ka_size)
        return lax.rem(pb_me + offset, pb_size)

    barrier = pltpu.get_barrier_semaphore()
    for axis, size in (("ka", ka_size), ("pb", pb_size)):
        for offset in range(1, size):
            pl.semaphore_signal(
                barrier,
                inc=1,
                device_id={axis: peer_of(axis, offset)},
                device_id_type=pl.DeviceIdType.MESH,
            )

    def begin(axis, phase, source_of, target):
        size, send, recv = (
            (ka_size, ka_send, ka_recv) if axis == "ka" else (pb_size, pb_send, pb_recv)
        )
        copies = []
        for offset in range(1, size):
            peer = peer_of(axis, offset)
            copy = pltpu.make_async_remote_copy(
                src_ref=source_of(peer),
                dst_ref=target,
                send_sem=send.at[phase, offset],
                recv_sem=recv.at[phase, offset],
                device_id={axis: peer},
                device_id_type=pl.DeviceIdType.MESH,
            )
            copy.start()
            copies.append(copy)
        return copies

    def pair(phase, peer, source, target):
        copy = pltpu.make_async_remote_copy(
            src_ref=source,
            dst_ref=target,
            send_sem=pair_send.at[phase],
            recv_sem=pair_recv.at[phase],
            device_id={"pb": peer},
            device_id_type=pl.DeviceIdType.MESH,
        )
        copy.start()
        return copy

    def finish(copies):
        for copy in copies:
            copy.wait()

    def load(number):
        source = pl.ds(pl.multiple_of(lax.rem(pb_me + number, pb_size) * block, block), block)
        return (
            pltpu.make_async_copy(keys_hbm.at[source], keys_v.at[number], load_sems.at[0, number]),
            pltpu.make_async_copy(
                values_hbm.at[source], values_v.at[number], load_sems.at[1, number]
            ),
        )

    for number in range(pb_size):
        for copy in load(number):
            copy.start()

    queries_all[pb_me] = queries_ref[...]
    own_wide = wide_queries(queries_ref[...] * exponent_scale)

    def pack(target, top, total):
        for piece in range(pieces):
            lanes = slice(piece * 128, (piece + 1) * 128)
            target[piece : piece + 1, :] = top[:, lanes]
            target[pieces + piece : pieces + piece + 1, :] = total[:, lanes]

    def unpack(value):
        return jnp.concatenate([value[piece : piece + 1] for piece in range(pieces)], axis=1)

    def target_block(number, carry):
        for copy in load(number):
            copy.wait()
        scores = product(wide_keys(keys_v[number]), own_wide, 1, 1)
        block_top = jnp.max(scores, axis=0, keepdims=True)
        turned = jnp.concatenate(halves(values_v[number].T), axis=0)
        if carry is None:
            top_next = block_top
        else:
            top, total = carry
            top_next = jnp.maximum(top, block_top)
            factor = jnp.exp2(top - top_next)
        exponent = jnp.exp2(scores - top_next)
        block_total = jnp.sum(exponent, axis=0, keepdims=True)
        added = product(
            jnp.concatenate((turned, turned), axis=1),
            jnp.concatenate(halves(exponent), axis=0),
        )
        if carry is None:
            sums[...] = added
            return top_next, block_total
        sums[...] = sums[...] * factor + added
        return top_next, total * factor + block_total

    carry = target_block(0, None)

    place = index_ref[pl.ds(pb_me, 1), :] - (ka_me * cache_rows + pb_me * block)
    place = jnp.broadcast_to(place.astype(jnp.float32), (group, group)).T
    first_row = lax.broadcasted_iota(jnp.int32, (group, group), 0) * stride
    offset_row = place - first_row.astype(jnp.float32)
    kept = jnp.zeros((group, width), jnp.float32)
    for step in range(stride):
        kept = jnp.where(
            offset_row == float(step), keys_v[0, pl.ds(step, group, stride=stride), :], kept
        )
    kept_all[ka_me] = kept

    pl.semaphore_wait(barrier, ka_size + pb_size - 2)
    query_copies = begin("pb", 0, lambda peer: queries_all.at[pb_me], queries_all.at[pb_me])
    kept_copies = begin("ka", 0, lambda peer: kept_all.at[ka_me], kept_all.at[ka_me])

    top, total = lax.fori_loop(1, pb_size, target_block, carry)
    part[...] = (sums[:width] + sums[width:]).reshape(ka_size, columns, query_rows)
    pack(stats, top, total)
    part_copies = begin("ka", 1, lambda peer: part.at[peer], part_in.at[ka_me])
    stats_copies = begin("ka", 2, lambda peer: stats, stats_in.at[ka_me])
    part_in[ka_me] = part[ka_me]
    stats_in[ka_me] = stats[...]

    finish(query_copies)
    finish(kept_copies)
    kept_wide = wide_keys(kept_all[...].reshape(ka_size * group, width))

    @pl.loop(0, pb_size)
    def _(number):
        queries_wide[...] = wide_queries(queries_all[number] * exponent_scale)
        scores = product(kept_wide, queries_wide[...], 1, 1)
        top = jnp.max(scores, axis=0, keepdims=True)
        exponent = jnp.exp2(scores - top)
        pack(kept_stats.at[pb_me, number], top, jnp.sum(exponent, axis=0, keepdims=True))
        one, two = halves(exponent)
        first_part[number] = one
        second_part[number] = two

    kept_stats_copies = begin("pb", 1, lambda peer: kept_stats.at[pb_me], kept_stats.at[pb_me])

    finish(stats_copies)
    finish(part_copies)
    joint_top = stats_in[0, :pieces]
    for source in range(1, ka_size):
        joint_top = jnp.maximum(joint_top, stats_in[source, :pieces])
    joint_total = jnp.zeros_like(joint_top)
    numerator = jnp.zeros((columns, query_rows), jnp.float32)
    for source in range(ka_size):
        factor = jnp.exp2(stats_in[source, :pieces] - joint_top)
        joint_total = joint_total + stats_in[source, pieces:] * factor
        numerator = numerator + part_in[source] * unpack(factor)
    target_all[pb_me] = numerator / unpack(joint_total)
    target_copies = begin("pb", 2, lambda peer: target_all.at[pb_me], target_all.at[pb_me])

    finish(kept_stats_copies)
    for number in range(pb_size):
        joint_top = kept_stats[0, number, :pieces]
        for source in range(1, pb_size):
            joint_top = jnp.maximum(joint_top, kept_stats[source, number, :pieces])
        joint_total = jnp.zeros_like(joint_top)
        for source in range(pb_size):
            joint_total = joint_total + kept_stats[source, number, pieces:] * jnp.exp2(
                kept_stats[source, number, :pieces] - joint_top
            )
        own_top = kept_stats[pb_me, number, :pieces]
        scale[number] = jnp.broadcast_to(
            unpack(jnp.exp2(own_top - joint_top) / joint_total), (columns, query_rows)
        )

    def backward(vectors):
        result = None
        for number in range(pb_size):
            rows = stacked(scale[number] * vectors(number))
            term = product(rows, first_part[number], 1, 1) + product(
                rows, second_part[number], 1, 1
            )
            result = term if result is None else result + term
        return folded(result)

    lane = lax.broadcasted_iota(jnp.int32, (columns, 128), 1)

    def forward(vector, tail):
        rows = stacked(vector)

        @pl.loop(0, 2)
        def _(half):
            for number in range(2):
                chunk = 2 * half + number
                term = folded(product(rows, first_part[chunk]) + product(rows, second_part[chunk]))
                half_out[half, :, number * query_rows : (number + 1) * query_rows] = (
                    scale[chunk] * term
                )
            half_out[half, :, half_width:] = tail

    def reduced(phase, slot):
        pair(phase, core_peer, half_out.at[1 - core_bit], core_in.at[slot]).wait()
        side_out[slot] = half_out[core_bit] + core_in[slot]
        pair(phase + 1, side_peer, side_out.at[slot], side_in.at[slot]).wait()
        return side_out[slot] + side_in[slot]

    def lane_sums(value):
        return jnp.sum(value, axis=1, keepdims=True)

    finish(target_copies)
    residual = backward(lambda number: target_all[number])
    residual_v[...] = residual
    forward(residual, jnp.where(lane == 0, lane_sums(residual * residual), 0.0))
    updates_all[core_bit] = reduced(0, 0)
    pair(2, core_peer, updates_all.at[core_bit], updates_all.at[core_bit]).wait()

    def updates_of(number):
        lanes = slice((number % 2) * query_rows, (number % 2 + 1) * query_rows)
        return updates_all[number // 2, :, lanes]

    norm_first = updates_all[0, :, half_width : half_width + 1]
    energy = lane_sums(updates_all[0, :, :half_width] * updates_all[0, :, :half_width])
    energy = energy + lane_sums(updates_all[1, :, :half_width] * updates_all[1, :, :half_width])
    step_first = norm_first / (energy + ridge_weight * norm_first)
    residual = residual_v[...]
    image = backward(updates_of) + ridge_weight * residual
    after = residual - step_first * image
    tail = jnp.where(
        lane == 0,
        lane_sums(after * after),
        jnp.where(lane == 1, lane_sums(after * residual), 0.0),
    )
    forward(after, tail)
    joined = reduced(3, 1)
    norm_second = joined[:, half_width : half_width + 1]
    cross = joined[:, half_width + 1 : half_width + 2]
    ratio = norm_second / norm_first
    updates = joined[:, :half_width] + ratio * updates_all[core_bit, :, :half_width]
    energy_out[...] = jnp.broadcast_to(lane_sums(updates * updates), energy_out.shape)
    pair(5, core_peer, energy_out, energy_in).wait()
    energy = energy_out[:, :1] + energy_in[:, :1]
    length = norm_second + 2.0 * ratio * cross + ratio * ratio * norm_first
    step_second = norm_second / (energy + ridge_weight * length)
    fitted = (step_first + step_second * ratio) * residual + step_second * after
    for target in range(ka_size):
        piece_out[target] = fitted[:, target * group : (target + 1) * group]
    piece_copies = begin("ka", 3, lambda peer: piece_out.at[peer], piece_in.at[ka_me])
    piece_in[ka_me] = piece_out[ka_me]
    finish(piece_copies)
    output_all[pb_me] = piece_in[...].reshape(width, group).T
    finish(begin("pb", 3, lambda peer: output_all.at[pb_me], output_all.at[pb_me]))
    fitted_ref[...] = output_all[...].reshape(pb_size * group, width)


def whole(queries, cache_keys, cache_values, kept_index, exponent_scale):
    ka_size, pb_size = lax.axis_size("ka"), lax.axis_size("pb")
    query_rows, width = queries.shape
    kept_rows = kept_index.shape[0]
    cache_rows = cache_keys.shape[0]
    group, block, columns = kept_rows // pb_size, cache_rows // pb_size, width // ka_size
    pieces = query_rows // 128
    joint = ka_size * group
    half_width = 2 * query_rows + 128
    space = functools.partial(pltpu.VMEM, dtype=jnp.float32)
    narrow = functools.partial(pltpu.VMEM, dtype=jnp.bfloat16)
    return pl.pallas_call(
        functools.partial(whole_kernel, ka_size, pb_size, exponent_scale),
        out_shape=jax.ShapeDtypeStruct((kept_rows, width), jnp.float32),
        in_specs=[pl.BlockSpec(memory_space=pltpu.VMEM)] * 2
        + [pl.BlockSpec(memory_space=pl.ANY)] * 2,
        out_specs=pl.BlockSpec(memory_space=pltpu.VMEM),
        scratch_shapes=[
            space((pb_size, block, width)),
            space((pb_size, block, width)),
            space((2 * width, query_rows)),
            space((pb_size, query_rows, width)),
            narrow((query_rows, 6 * width)),
            space((ka_size, group, width)),
            space((ka_size, columns, query_rows)),
            space((ka_size, columns, query_rows)),
            space((2 * pieces, 128)),
            space((ka_size, 2 * pieces, 128)),
            narrow((pb_size, joint, query_rows)),
            narrow((pb_size, joint, query_rows)),
            space((pb_size, pb_size, 2 * pieces, 128)),
            space((pb_size, columns, query_rows)),
            space((pb_size, columns, query_rows)),
            space((columns, joint)),
            space((2, columns, half_width)),
            space((2, columns, half_width)),
            space((2, columns, half_width)),
            space((2, columns, half_width)),
            space((2, columns, half_width)),
            space((columns, 128)),
            space((columns, 128)),
            space((ka_size, columns, group)),
            space((ka_size, columns, group)),
            space((pb_size, group, width)),
            pltpu.SemaphoreType.DMA((2, pb_size)),
            pltpu.SemaphoreType.DMA((4, ka_size)),
            pltpu.SemaphoreType.DMA((4, ka_size)),
            pltpu.SemaphoreType.DMA((4, pb_size)),
            pltpu.SemaphoreType.DMA((4, pb_size)),
            pltpu.SemaphoreType.DMA((6,)),
            pltpu.SemaphoreType.DMA((6,)),
        ],
        compiler_params=pltpu.CompilerParams(
            collective_id=1, has_side_effects=True, vmem_limit_bytes=56 * 1024 * 1024
        ),
    )(queries, kept_index.reshape(pb_size, group), cache_keys, cache_values)


def suits(ka_size, pb_size, queries, cache_keys, kept_index):
    width = queries.shape[1]
    group = kept_index.shape[0] // pb_size
    return (
        pb_size == 4
        and width == 128
        and group == 128
        and queries.shape[0] == 512
        and cache_keys.shape[0] == 8192
        and width % (8 * ka_size) == 0
    )


def shards(queries, cache_keys, cache_values, kept_index):
    head_width = queries.shape[1]
    inverse_root = 1.0 / math.sqrt(head_width)
    cache_rows = cache_keys.shape[0]
    if suits(lax.axis_size("ka"), lax.axis_size("pb"), queries, cache_keys, kept_index):
        exponent_scale = inverse_root * math.log2(math.e)
        return whole(queries, cache_keys, cache_values, kept_index, exponent_scale)

    local_kept = kept_index - lax.axis_index("ka") * cache_rows
    kept_keys = jnp.take(cache_keys, local_kept, axis=0)
    kept_scores = contract(queries, kept_keys, 1, 1) * inverse_root
    kept_top = jnp.max(kept_scores, axis=1)
    kept_exponent = jnp.exp(kept_scores - kept_top[:, None])
    kept_total = jnp.sum(kept_exponent, axis=1)

    zero = jnp.zeros_like(kept_top)
    stats = jnp.stack((zero, zero, kept_top, kept_total), axis=1)
    stats = jnp.pad(stats, ((0, 0), (0, head_width - 4)))
    return fit(
        target_part(queries, cache_keys, cache_values, stats, inverse_root), kept_exponent
    )


def solution(mesh):
    in_specs = (P("pb", None), P("ka", None), P("ka", None), P("ka"))
    out_specs = P("ka", None)
    return jax.shard_map(shards, mesh=mesh, in_specs=in_specs, out_specs=out_specs, check_vma=False)
```

```python
import functools
import math

import jax
import jax.numpy as jnp
from jax import lax
from jax.experimental import pallas as pl
from jax.experimental.pallas import tpu as pltpu
from jax.sharding import PartitionSpec as P

ITERS = 2


ridge_weight = 0.01
highest = lax.Precision.HIGHEST


def contract(left_side, right_side, left_dim, right_dim):
    return lax.dot_general(
        left_side,
        right_side,
        (((left_dim,), (right_dim,)), ((), ())),
        precision=highest,
        preferred_element_type=jnp.float32,
    )


def column_sums(left_side, right_side):
    return jnp.sum(left_side * right_side, axis=0, keepdims=True)


def fit_kernel(
    ka_size,
    pb_size,
    part_ref,
    kept_ref,
    fitted_ref,
    flipped,
    stats_in,
    stats_all,
    ka_out,
    ka_in,
    ka_all,
    pb_out,
    pb_in,
    pb_all,
    tail_out,
    tail_in,
    ka_send,
    ka_recv,
    pb_send,
    pb_recv,
):
    ka_me = lax.axis_index("ka")
    pb_me = lax.axis_index("pb")
    width = fitted_ref.shape[1]
    query_rows = kept_ref.shape[0]
    kept_rows = kept_ref.shape[1]
    ka_share = query_rows // ka_size
    pb_share = kept_rows // pb_size

    def peer_of(axis, offset):
        size = ka_size if axis == "ka" else pb_size
        me = ka_me if axis == "ka" else pb_me
        return lax.rem(me + offset, size)

    barrier = pltpu.get_barrier_semaphore()
    for axis, size in (("ka", ka_size), ("pb", pb_size)):
        for offset in range(1, size):
            pl.semaphore_signal(
                barrier,
                inc=1,
                device_id={axis: peer_of(axis, offset)},
                device_id_type=pl.DeviceIdType.MESH,
            )
    pl.semaphore_wait(barrier, ka_size + pb_size - 2)

    def begin(axis, phase, source_of, target):
        size, send, recv = (
            (ka_size, ka_send, ka_recv) if axis == "ka" else (pb_size, pb_send, pb_recv)
        )
        copies = []
        for offset in range(1, size):
            peer = peer_of(axis, offset)
            copy = pltpu.make_async_remote_copy(
                src_ref=source_of(peer),
                dst_ref=target,
                send_sem=send.at[phase, offset],
                recv_sem=recv.at[phase, offset],
                device_id={axis: peer},
                device_id_type=pl.DeviceIdType.MESH,
            )
            copy.start()
            copies.append(copy)
        return copies

    def finish(copies):
        for copy in copies:
            copy.wait()

    def scattered_sum(axis, phase, value, tail, out, arrived, whole):
        me, size, share = (
            (ka_me, ka_size, ka_share) if axis == "ka" else (pb_me, pb_size, pb_share)
        )
        out[:, :share, :] = value.reshape(size, share, width)
        out[:, share:, :] = jnp.broadcast_to(tail[None], (size, 8, width))
        copies = begin(axis, phase, lambda peer: out.at[peer], arrived.at[me])
        arrived[me] = out[me]
        finish(copies)
        total = arrived[0]
        for source in range(1, size):
            total = total + arrived[source]
        whole[me] = total[:share]
        finish(begin(axis, phase + 1, lambda peer: whole.at[me], whole.at[me]))
        return whole[...].reshape(size * share, width), total[share:]

    def matmul(left_side, right_side):
        return jnp.dot(
            left_side, right_side, precision=highest, preferred_element_type=jnp.float32
        )

    def tail_rows(*rows):
        place = lax.broadcasted_iota(jnp.int32, (8, width), 0)
        tail = jnp.zeros((8, width), jnp.float32)
        for number, row in enumerate(rows):
            tail = jnp.where(place == number, row, tail)
        return tail

    copies = begin("ka", 0, lambda peer: part_ref.at[peer], stats_in.at[ka_me])
    stats_in[ka_me] = part_ref[ka_me]
    flipped[...] = kept_ref[...].T
    finish(copies)

    def column(source, number):
        return stats_in[source, :, width + number : width + number + 1]

    top = column(0, 0)
    kept_top = column(0, 2)
    for source in range(1, ka_size):
        top = jnp.maximum(top, column(source, 0))
        kept_top = jnp.maximum(kept_top, column(source, 2))
    total = jnp.zeros_like(top)
    kept_total = jnp.zeros_like(top)
    numerator = jnp.zeros((ka_share, width), jnp.float32)
    for source in range(ka_size):
        factor = jnp.exp(column(source, 0) - top)
        total = total + column(source, 1) * factor
        numerator = numerator + stats_in[source, :, :width] * factor
        kept_total = kept_total + column(source, 3) * jnp.exp(column(source, 2) - kept_top)
    lane = lax.broadcasted_iota(jnp.int32, (ka_share, width), 1)
    stats_all[ka_me, :, :width] = numerator / total
    stats_all[ka_me, :, width:] = jnp.where(lane == 0, kept_top, kept_total)
    finish(begin("ka", 1, lambda peer: stats_all.at[ka_me], stats_all.at[ka_me]))
    target = stats_all[:, :, :width].reshape(query_rows, width)
    joint_top = stats_all[:, :, width : width + 1].reshape(query_rows, 1)
    joint_total = stats_all[:, :, width + 1 : width + 2].reshape(query_rows, 1)
    own_top = part_ref[:, :, width + 2 : width + 3].reshape(query_rows, 1)
    scale = jnp.exp(own_top - joint_top) / joint_total

    no_tail = jnp.zeros((8, width), jnp.float32)
    residual, _ = scattered_sum(
        "pb",
        0,
        matmul(flipped[...], scale * target),
        no_tail,
        pb_out.at[0],
        pb_in.at[0],
        pb_all.at[0],
    )
    fitted = jnp.zeros_like(residual)
    direction = residual
    updates = None
    norm_now = None
    length_now = None
    for iteration in range(ITERS):
        forward = scale * matmul(kept_ref[...], residual)
        tail = tail_rows(column_sums(residual, residual), column_sums(residual, direction))
        summed, tail = scattered_sum(
            "ka",
            2 + 2 * iteration,
            forward,
            tail,
            ka_out.at[iteration],
            ka_in.at[iteration],
            ka_all.at[iteration],
        )
        norm_next = tail[0:1]
        if iteration == 0:
            updates = summed
            length_now = norm_next
        else:
            ratio = norm_next / norm_now
            direction = residual + ratio * direction
            updates = summed + ratio * updates
            length_now = norm_next + 2.0 * ratio * tail[1:2] + ratio * ratio * length_now
        norm_now = norm_next
        energy = tail_rows(column_sums(updates, updates))
        if iteration + 1 == ITERS:
            tail_out[...] = energy
            copies = begin("pb", 2 * ITERS, lambda peer: tail_out, tail_in.at[pb_me])
            tail_in[pb_me] = energy
            finish(copies)
            energy = tail_in[0]
            for source in range(1, pb_size):
                energy = energy + tail_in[source]
            step_length = norm_now / (energy[0:1] + ridge_weight * length_now)
            fitted_ref[...] = fitted + step_length * direction
        else:
            image, energy = scattered_sum(
                "pb",
                2 + 2 * iteration,
                matmul(flipped[...], scale * updates),
                energy,
                pb_out.at[iteration + 1],
                pb_in.at[iteration + 1],
                pb_all.at[iteration + 1],
            )
            step_length = norm_now / (energy[0:1] + ridge_weight * length_now)
            fitted = fitted + step_length * direction
            residual = residual - step_length * (image + ridge_weight * direction)


def fit(part, kept_exponent):
    ka_size, pb_size = lax.axis_size("ka"), lax.axis_size("pb")
    query_rows, kept_rows = kept_exponent.shape
    width = part.shape[1] // 2
    ka_share, pb_share = query_rows // ka_size, kept_rows // pb_size
    space = functools.partial(pltpu.VMEM, dtype=jnp.float32)
    return pl.pallas_call(
        functools.partial(fit_kernel, ka_size, pb_size),
        out_shape=jax.ShapeDtypeStruct((kept_rows, width), jnp.float32),
        in_specs=[pl.BlockSpec(memory_space=pltpu.VMEM)] * 2,
        out_specs=pl.BlockSpec(memory_space=pltpu.VMEM),
        scratch_shapes=[
            space((kept_rows, query_rows)),
            space((ka_size, ka_share, 2 * width)),
            space((ka_size, ka_share, 2 * width)),
            space((ITERS, ka_size, ka_share + 8, width)),
            space((ITERS, ka_size, ka_share + 8, width)),
            space((ITERS, ka_size, ka_share, width)),
            space((ITERS, pb_size, pb_share + 8, width)),
            space((ITERS, pb_size, pb_share + 8, width)),
            space((ITERS, pb_size, pb_share, width)),
            space((8, width)),
            space((pb_size, 8, width)),
            pltpu.SemaphoreType.DMA((2 + 2 * ITERS, ka_size)),
            pltpu.SemaphoreType.DMA((2 + 2 * ITERS, ka_size)),
            pltpu.SemaphoreType.DMA((2 * ITERS + 1, pb_size)),
            pltpu.SemaphoreType.DMA((2 * ITERS + 1, pb_size)),
        ],
        compiler_params=pltpu.CompilerParams(
            collective_id=0, has_side_effects=True, vmem_limit_bytes=40 * 1024 * 1024
        ),
    )(part.reshape(ka_size, ka_share, 2 * width), kept_exponent)


def thirds(value):
    first = value.astype(jnp.bfloat16)
    rest = value - first.astype(jnp.float32)
    second = rest.astype(jnp.bfloat16)
    third = (rest - second.astype(jnp.float32)).astype(jnp.bfloat16)
    return first, second, third


def target_kernel(inverse_root, queries_ref, keys_ref, values_ref, kept_ref, part_ref, wide, top, total, sums):
    width = queries_ref.shape[1]

    @pl.when(pl.program_id(0) == 0)
    def _():
        one, two, three = thirds(queries_ref[...])
        wide[...] = jnp.concatenate((one, one, two, one, three, two), axis=1)
        top[...] = jnp.full_like(top, -jnp.inf)
        total[...] = jnp.zeros_like(total)
        sums[...] = jnp.zeros_like(sums)

    one, two, three = thirds(keys_ref[...])
    scores = (
        lax.dot_general(
            wide[...],
            jnp.concatenate((one, two, one, three, one, two), axis=1),
            (((1,), (1,)), ((), ())),
            preferred_element_type=jnp.float32,
        )
        * inverse_root
    )
    top_next = jnp.maximum(top[...], jnp.max(scores, axis=1, keepdims=True))
    factor = jnp.exp(top[...] - top_next)
    exponent = jnp.exp(scores - top_next)
    top[...] = top_next
    total[...] = total[...] * factor + jnp.sum(exponent, axis=1, keepdims=True)
    one, two, three = thirds(values_ref[...])
    high, middle, low = thirds(exponent)
    pair = jnp.concatenate((one, two), axis=1)
    product = functools.partial(jnp.dot, preferred_element_type=jnp.float32)
    both = product(high, pair) + product(middle, pair)
    small = product(high, three) + product(low, one)
    sums[...] = sums[...] * factor + (both[:, :width] + (both[:, width:] + small))

    @pl.when(pl.program_id(0) == pl.num_programs(0) - 1)
    def _():
        lane = lax.broadcasted_iota(jnp.int32, kept_ref.shape, 1)
        stats = jnp.where(lane == 0, top[...], jnp.where(lane == 1, total[...], kept_ref[...]))
        part_ref[:, :width] = sums[...]
        part_ref[:, width:] = stats


def target_part(queries, cache_keys, cache_values, kept_stats, inverse_root):
    query_rows, width = queries.shape
    block_size = min(2048, cache_keys.shape[0])
    fixed = pl.BlockSpec((query_rows, width), lambda block: (0, 0))
    moving = pl.BlockSpec((block_size, width), lambda block: (block, 0))
    return pl.pallas_call(
        functools.partial(target_kernel, inverse_root),
        grid=(cache_keys.shape[0] // block_size,),
        out_shape=jax.ShapeDtypeStruct((query_rows, 2 * width), jnp.float32),
        in_specs=[fixed, moving, moving, fixed],
        out_specs=pl.BlockSpec((query_rows, 2 * width), lambda block: (0, 0)),
        scratch_shapes=[
            pltpu.VMEM((query_rows, 6 * width), jnp.bfloat16),
            pltpu.VMEM((query_rows, 1), jnp.float32),
            pltpu.VMEM((query_rows, 1), jnp.float32),
            pltpu.VMEM((query_rows, width), jnp.float32),
        ],
        compiler_params=pltpu.CompilerParams(vmem_limit_bytes=40 * 1024 * 1024),
    )(queries, cache_keys, cache_values, kept_stats)


def halves(value):
    first = value.astype(jnp.bfloat16)
    return first, (value - first.astype(jnp.float32)).astype(jnp.bfloat16)


def product(left_side, right_side, left_dim=1, right_dim=0):
    return lax.dot_general(
        left_side,
        right_side,
        (((left_dim,), (right_dim,)), ((), ())),
        preferred_element_type=jnp.float32,
    )


def wide_queries(value):
    one, two, three = thirds(value)
    return jnp.concatenate((one, one, two, one, three, two), axis=1)


def wide_keys(value):
    one, two, three = thirds(value)
    return jnp.concatenate((one, two, one, three, one, two), axis=1)


def stacked(value):
    return jnp.concatenate(thirds(value), axis=0)


def folded(value):
    rows = value.shape[0] // 3
    return value[:rows] + (value[rows : 2 * rows] + value[2 * rows :])


def whole_kernel(
    ka_size,
    pb_size,
    exponent_scale,
    queries_ref,
    index_ref,
    keys_hbm,
    values_hbm,
    fitted_ref,
    keys_v,
    values_v,
    sums,
    queries_all,
    queries_wide,
    kept_all,
    part,
    part_in,
    stats,
    stats_in,
    first_part,
    second_part,
    kept_stats,
    scale,
    target_all,
    residual_v,
    half_out,
    core_in,
    side_out,
    side_in,
    updates_all,
    energy_out,
    energy_in,
    piece_out,
    piece_in,
    blocks_all,
    factors,
    load_sems,
    ka_send,
    ka_recv,
    pb_send,
    pb_recv,
    pair_send,
    pair_recv,
):
    ka_me = lax.axis_index("ka")
    pb_me = lax.axis_index("pb")
    query_rows, width = queries_ref.shape
    columns = width // ka_size
    pieces = query_rows // 128
    group = kept_all.shape[1]
    cache_rows = keys_hbm.shape[0]
    block = cache_rows // pb_size
    stride = block // group
    core_bit = lax.rem(pb_me, 2)
    core_peer = pb_me + 1 - 2 * core_bit
    side_peer = lax.rem(pb_me + 2, 4)

    def peer_of(axis, offset):
        if axis == "ka":
            return lax.rem(ka_me + offset, ka_size)
        return lax.rem(pb_me + offset, pb_size)

    barrier = pltpu.get_barrier_semaphore()
    for axis, size in (("ka", ka_size), ("pb", pb_size)):
        for offset in range(1, size):
            pl.semaphore_signal(
                barrier,
                inc=1,
                device_id={axis: peer_of(axis, offset)},
                device_id_type=pl.DeviceIdType.MESH,
            )

    def begin(axis, phase, source_of, target):
        size, send, recv = (
            (ka_size, ka_send, ka_recv) if axis == "ka" else (pb_size, pb_send, pb_recv)
        )
        copies = []
        for offset in range(1, size):
            peer = peer_of(axis, offset)
            copy = pltpu.make_async_remote_copy(
                src_ref=source_of(peer),
                dst_ref=target,
                send_sem=send.at[phase, offset],
                recv_sem=recv.at[phase, offset],
                device_id={axis: peer},
                device_id_type=pl.DeviceIdType.MESH,
            )
            copy.start()
            copies.append(copy)
        return copies

    def pair(phase, peer, source, target):
        copy = pltpu.make_async_remote_copy(
            src_ref=source,
            dst_ref=target,
            send_sem=pair_send.at[phase],
            recv_sem=pair_recv.at[phase],
            device_id={"pb": peer},
            device_id_type=pl.DeviceIdType.MESH,
        )
        copy.start()
        return copy

    def finish(copies):
        for copy in copies:
            copy.wait()

    def load(number):
        source = pl.ds(pl.multiple_of(lax.rem(pb_me + number, pb_size) * block, block), block)
        return (
            pltpu.make_async_copy(keys_hbm.at[source], keys_v.at[number], load_sems.at[0, number]),
            pltpu.make_async_copy(
                values_hbm.at[source], values_v.at[number], load_sems.at[1, number]
            ),
        )

    for number in range(pb_size):
        for copy in load(number):
            copy.start()

    queries_all[pb_me] = queries_ref[...]
    own_wide = wide_queries(queries_ref[...] * exponent_scale)

    def pack(target, top, total):
        for piece in range(pieces):
            lanes = slice(piece * 128, (piece + 1) * 128)
            target[piece : piece + 1, :] = top[:, lanes]
            target[pieces + piece : pieces + piece + 1, :] = total[:, lanes]

    def unpack(value):
        return jnp.concatenate([value[piece : piece + 1] for piece in range(pieces)], axis=1)

    load(0)[0].wait()
    place = index_ref[pl.ds(pb_me, 1), :] - (ka_me * cache_rows + pb_me * block)
    place = jnp.broadcast_to(place.astype(jnp.float32), (group, group)).T
    first_row = lax.broadcasted_iota(jnp.int32, (group, group), 0) * stride
    offset_row = place - first_row.astype(jnp.float32)
    kept = jnp.zeros((group, width), jnp.float32)
    for step in range(stride):
        kept = jnp.where(
            offset_row == float(step), keys_v[0, pl.ds(step, group, stride=stride), :], kept
        )
    kept_all[ka_me] = kept

    pl.semaphore_wait(barrier, ka_size + pb_size - 2)
    kept_copies = begin("ka", 0, lambda peer: kept_all.at[ka_me], kept_all.at[ka_me])
    query_copies = begin("pb", 0, lambda peer: queries_all.at[pb_me], queries_all.at[pb_me])

    def target_block(number, carry):
        keys_load, values_load = load(number)
        if carry is None:
            scores = product(wide_keys(keys_v[number]), own_wide, 1, 1)
            top_next = jnp.max(scores, axis=0, keepdims=True)
        else:
            keys_load.wait()
            scores = product(wide_keys(keys_v[number]), own_wide, 1, 1)
            top, total = carry
            top_next = jnp.maximum(top, jnp.max(scores, axis=0, keepdims=True))
            factor = jnp.exp2(top - top_next)
        values_load.wait()
        turned = jnp.concatenate(halves(values_v[number].T), axis=0)
        exponent = jnp.exp2(scores - top_next)
        block_total = jnp.sum(exponent, axis=0, keepdims=True)
        added = product(
            jnp.concatenate((turned, turned), axis=1),
            jnp.concatenate(halves(exponent), axis=0),
        )
        if carry is None:
            sums[...] = added
            return top_next, block_total
        sums[...] = sums[...] * factor + added
        return top_next, total * factor + block_total

    top, total = lax.fori_loop(1, pb_size, target_block, target_block(0, None))
    part[...] = (sums[:width] + sums[width:]).reshape(ka_size, columns, query_rows)
    pack(stats, top, total)
    part_copies = begin("ka", 1, lambda peer: part.at[peer], part_in.at[ka_me])
    stats_copies = begin("ka", 2, lambda peer: stats, stats_in.at[ka_me])
    part_in[ka_me] = part[ka_me]
    stats_in[ka_me] = stats[...]

    finish(query_copies)
    finish(kept_copies)
    kept_wide = wide_keys(kept_all[...].reshape(ka_size * group, width))

    @pl.loop(0, pb_size)
    def _(number):
        queries_wide[...] = wide_queries(queries_all[number] * exponent_scale)
        scores = product(kept_wide, queries_wide[...], 1, 1)
        top = jnp.max(scores, axis=0, keepdims=True)
        exponent = jnp.exp2(scores - top)
        pack(kept_stats.at[pb_me, number], top, jnp.sum(exponent, axis=0, keepdims=True))
        one, two = halves(exponent)
        first_part[number] = one
        second_part[number] = two

    kept_stats_copies = begin("pb", 1, lambda peer: kept_stats.at[pb_me], kept_stats.at[pb_me])

    finish(stats_copies)
    finish(part_copies)
    joint_top = stats_in[0, :pieces]
    for source in range(1, ka_size):
        joint_top = jnp.maximum(joint_top, stats_in[source, :pieces])
    joint_total = jnp.zeros_like(joint_top)
    numerator = jnp.zeros((columns, query_rows), jnp.float32)
    for source in range(ka_size):
        factor = jnp.exp2(stats_in[source, :pieces] - joint_top)
        joint_total = joint_total + stats_in[source, pieces:] * factor
        numerator = numerator + part_in[source] * unpack(factor)
    target_all[pb_me] = numerator / unpack(joint_total)
    target_copies = begin("pb", 2, lambda peer: target_all.at[pb_me], target_all.at[pb_me])

    finish(kept_stats_copies)
    for number in range(pb_size):
        joint_top = kept_stats[0, number, :pieces]
        for source in range(1, pb_size):
            joint_top = jnp.maximum(joint_top, kept_stats[source, number, :pieces])
        joint_total = jnp.zeros_like(joint_top)
        for source in range(pb_size):
            joint_total = joint_total + kept_stats[source, number, pieces:] * jnp.exp2(
                kept_stats[source, number, :pieces] - joint_top
            )
        own_top = kept_stats[pb_me, number, :pieces]
        scale[number] = jnp.broadcast_to(
            unpack(jnp.exp2(own_top - joint_top) / joint_total), (columns, query_rows)
        )

    def backward(number, vector):
        rows = stacked(scale[number] * vector)
        return product(rows, first_part[number], 1, 1) + product(rows, second_part[number], 1, 1)

    lane = lax.broadcasted_iota(jnp.int32, (columns, 128), 1)

    def lane_sums(value):
        return jnp.sum(value, axis=1, keepdims=True)

    def long(number):
        return query_rows + 128 if number == 0 else query_rows

    def forward(phase, slot, vector, tail):
        rows = stacked(vector)

        def chunk_of(half, number):
            chunk = 2 * half + number
            term = folded(product(rows, first_part[chunk]) + product(rows, second_part[chunk]))
            half_out[slot, half, number, :, :query_rows] = scale[chunk] * term
            if number == 0:
                half_out[slot, half, number, :, query_rows:] = tail

        core_copies = []
        for number in range(2):
            chunk_of(1 - core_bit, number)
            lanes = pl.ds(0, long(number))
            core_copies.append(
                pair(
                    phase + number,
                    core_peer,
                    half_out.at[slot, 1 - core_bit, number, :, lanes],
                    core_in.at[slot, number, :, lanes],
                )
            )
        side_copies = []
        for number in range(2):
            chunk_of(core_bit, number)
            core_copies[number].wait()
            lanes = pl.ds(0, long(number))
            side_out[slot, number, :, lanes] = (
                half_out[slot, core_bit, number, :, lanes] + core_in[slot, number, :, lanes]
            )
            side_copies.append(
                pair(
                    phase + 2 + number,
                    side_peer,
                    side_out.at[slot, number, :, lanes],
                    side_in.at[slot, number, :, lanes],
                )
            )
        return side_copies

    def spread(phase, slot, value):
        for target in range(ka_size):
            piece_out[slot, target] = value[:, target * group : (target + 1) * group]
        piece_in[slot, ka_me] = piece_out[slot, ka_me]
        return begin(
            "ka", phase, lambda peer: piece_out.at[slot, peer], piece_in.at[slot, ka_me]
        )

    def share(phase, slot):
        blocks_all[slot, pb_me] = piece_in[slot].reshape(width, group)
        return begin(
            "pb", phase, lambda peer: blocks_all.at[slot, pb_me], blocks_all.at[slot, pb_me]
        )

    image = backward(pb_me, target_all[pb_me])
    for offset in (1, 3, 2):
        target_copies[offset - 1].wait()
        source = lax.rem(pb_me + pb_size - offset, pb_size)
        image = image + backward(source, target_all[source])
    residual = folded(image)
    residual_v[...] = residual
    side_copies = forward(
        0, 0, residual, jnp.where(lane == 0, lane_sums(residual * residual), 0.0)
    )
    spread_copies = spread(3, 0, residual)
    update_copies = []
    for number in range(2):
        side_copies[number].wait()
        joined = side_out[0, number, :, :query_rows] + side_in[0, number, :, :query_rows]
        updates_all[2 * core_bit + number] = joined
        update_copies.append(
            pair(
                4 + number,
                core_peer,
                updates_all.at[2 * core_bit + number],
                updates_all.at[2 * core_bit + number],
            )
        )
    norm_first = (side_out[0, 0, :, query_rows:] + side_in[0, 0, :, query_rows:])[:, :1]
    image = None
    energy = None
    for half in (core_bit, 1 - core_bit):
        for number in range(2):
            if half is not core_bit:
                update_copies[number].wait()
            updates = updates_all[2 * half + number]
            term = backward(2 * half + number, updates)
            image = term if image is None else image + term
            term = lane_sums(updates * updates)
            energy = term if energy is None else energy + term
        if half is core_bit:
            finish(spread_copies)
            first_copies = share(3, 0)
    step_first = norm_first / (energy + ridge_weight * norm_first)
    residual = residual_v[...]
    after = residual - step_first * (folded(image) + ridge_weight * residual)
    spread_copies = spread(4, 1, after)
    tail = jnp.where(
        lane == 0,
        lane_sums(after * after),
        jnp.where(lane == 1, lane_sums(after * residual), 0.0),
    )
    side_copies = forward(6, 1, after, tail)
    finish(side_copies)
    tail = side_out[1, 0, :, query_rows:] + side_in[1, 0, :, query_rows:]
    norm_second = tail[:, :1]
    ratio = norm_second / norm_first
    energy = None
    for number in range(2):
        updates = side_out[1, number, :, :query_rows] + side_in[1, number, :, :query_rows]
        updates = updates + ratio * updates_all[2 * core_bit + number]
        term = lane_sums(updates * updates)
        energy = term if energy is None else energy + term
    energy_out[...] = jnp.broadcast_to(energy, energy_out.shape)
    energy_copy = pair(10, core_peer, energy_out, energy_in)
    finish(spread_copies)
    second_copies = share(4, 1)
    energy_copy.wait()
    energy = energy_out[:, :1] + energy_in[:, :1]
    length = norm_second + 2.0 * ratio * tail[:, 1:2] + ratio * ratio * norm_first
    step_second = norm_second / (energy + ridge_weight * length)
    factors[ka_me] = jnp.where(lane == 0, step_first + step_second * ratio, step_second)
    factor_copies = begin("ka", 5, lambda peer: factors.at[ka_me], factors.at[ka_me])
    finish(first_copies)
    finish(second_copies)
    turned = [[blocks_all[slot, number].T for number in range(pb_size)] for slot in range(2)]
    finish(factor_copies)
    both = factors[...].reshape(width, 128).T
    for number in range(pb_size):
        fitted_ref[number * group : (number + 1) * group, :] = (
            both[0:1] * turned[0][number] + both[1:2] * turned[1][number]
        )


def whole(queries, cache_keys, cache_values, kept_index, exponent_scale):
    ka_size, pb_size = lax.axis_size("ka"), lax.axis_size("pb")
    query_rows, width = queries.shape
    kept_rows = kept_index.shape[0]
    cache_rows = cache_keys.shape[0]
    group, block, columns = kept_rows // pb_size, cache_rows // pb_size, width // ka_size
    pieces = query_rows // 128
    joint = ka_size * group
    space = functools.partial(pltpu.VMEM, dtype=jnp.float32)
    narrow = functools.partial(pltpu.VMEM, dtype=jnp.bfloat16)
    return pl.pallas_call(
        functools.partial(whole_kernel, ka_size, pb_size, exponent_scale),
        out_shape=jax.ShapeDtypeStruct((kept_rows, width), jnp.float32),
        in_specs=[pl.BlockSpec(memory_space=pltpu.VMEM)] * 2
        + [pl.BlockSpec(memory_space=pl.ANY)] * 2,
        out_specs=pl.BlockSpec(memory_space=pltpu.VMEM),
        scratch_shapes=[
            space((pb_size, block, width)),
            space((pb_size, block, width)),
            space((2 * width, query_rows)),
            space((pb_size, query_rows, width)),
            narrow((query_rows, 6 * width)),
            space((ka_size, group, width)),
            space((ka_size, columns, query_rows)),
            space((ka_size, columns, query_rows)),
            space((2 * pieces, 128)),
            space((ka_size, 2 * pieces, 128)),
            narrow((pb_size, joint, query_rows)),
            narrow((pb_size, joint, query_rows)),
            space((pb_size, pb_size, 2 * pieces, 128)),
            space((pb_size, columns, query_rows)),
            space((pb_size, columns, query_rows)),
            space((columns, joint)),
            space((2, 2, 2, columns, query_rows + 128)),
            space((2, 2, columns, query_rows + 128)),
            space((2, 2, columns, query_rows + 128)),
            space((2, 2, columns, query_rows + 128)),
            space((pb_size, columns, query_rows)),
            space((columns, 128)),
            space((columns, 128)),
            space((2, ka_size, columns, group)),
            space((2, ka_size, columns, group)),
            space((2, pb_size, width, group)),
            space((ka_size, columns, 128)),
            pltpu.SemaphoreType.DMA((2, pb_size)),
            pltpu.SemaphoreType.DMA((6, ka_size)),
            pltpu.SemaphoreType.DMA((6, ka_size)),
            pltpu.SemaphoreType.DMA((5, pb_size)),
            pltpu.SemaphoreType.DMA((5, pb_size)),
            pltpu.SemaphoreType.DMA((11,)),
            pltpu.SemaphoreType.DMA((11,)),
        ],
        compiler_params=pltpu.CompilerParams(
            collective_id=1, has_side_effects=True, vmem_limit_bytes=56 * 1024 * 1024
        ),
    )(queries, kept_index.reshape(pb_size, group), cache_keys, cache_values)


def suits(ka_size, pb_size, queries, cache_keys, kept_index):
    width = queries.shape[1]
    group = kept_index.shape[0] // pb_size
    return (
        pb_size == 4
        and width == 128
        and group == 128
        and queries.shape[0] == 512
        and cache_keys.shape[0] == 8192
        and width % (8 * ka_size) == 0
    )


def shards(queries, cache_keys, cache_values, kept_index):
    head_width = queries.shape[1]
    inverse_root = 1.0 / math.sqrt(head_width)
    cache_rows = cache_keys.shape[0]
    if suits(lax.axis_size("ka"), lax.axis_size("pb"), queries, cache_keys, kept_index):
        exponent_scale = inverse_root * math.log2(math.e)
        return whole(queries, cache_keys, cache_values, kept_index, exponent_scale)

    local_kept = kept_index - lax.axis_index("ka") * cache_rows
    kept_keys = jnp.take(cache_keys, local_kept, axis=0)
    kept_scores = contract(queries, kept_keys, 1, 1) * inverse_root
    kept_top = jnp.max(kept_scores, axis=1)
    kept_exponent = jnp.exp(kept_scores - kept_top[:, None])
    kept_total = jnp.sum(kept_exponent, axis=1)

    zero = jnp.zeros_like(kept_top)
    stats = jnp.stack((zero, zero, kept_top, kept_total), axis=1)
    stats = jnp.pad(stats, ((0, 0), (0, head_width - 4)))
    return fit(
        target_part(queries, cache_keys, cache_values, stats, inverse_root), kept_exponent
    )


def solution(mesh):
    in_specs = (P("pb", None), P("ka", None), P("ka", None), P("ka"))
    out_specs = P("ka", None)
    return jax.shard_map(shards, mesh=mesh, in_specs=in_specs, out_specs=out_specs, check_vma=False)
```

```python
import functools
import math

import jax
import jax.numpy as jnp
from jax import lax
from jax.experimental import pallas as pl
from jax.experimental.pallas import tpu as pltpu
from jax.sharding import PartitionSpec as P

ITERS = 2


ridge_weight = 0.01
highest = lax.Precision.HIGHEST


def contract(left_side, right_side, left_dim, right_dim):
    return lax.dot_general(
        left_side,
        right_side,
        (((left_dim,), (right_dim,)), ((), ())),
        precision=highest,
        preferred_element_type=jnp.float32,
    )


def column_sums(left_side, right_side):
    return jnp.sum(left_side * right_side, axis=0, keepdims=True)


def fit_kernel(
    ka_size,
    pb_size,
    part_ref,
    kept_ref,
    fitted_ref,
    flipped,
    stats_in,
    stats_all,
    ka_out,
    ka_in,
    ka_all,
    pb_out,
    pb_in,
    pb_all,
    tail_out,
    tail_in,
    ka_send,
    ka_recv,
    pb_send,
    pb_recv,
):
    ka_me = lax.axis_index("ka")
    pb_me = lax.axis_index("pb")
    width = fitted_ref.shape[1]
    query_rows = kept_ref.shape[0]
    kept_rows = kept_ref.shape[1]
    ka_share = query_rows // ka_size
    pb_share = kept_rows // pb_size

    def peer_of(axis, offset):
        size = ka_size if axis == "ka" else pb_size
        me = ka_me if axis == "ka" else pb_me
        return lax.rem(me + offset, size)

    barrier = pltpu.get_barrier_semaphore()
    for axis, size in (("ka", ka_size), ("pb", pb_size)):
        for offset in range(1, size):
            pl.semaphore_signal(
                barrier,
                inc=1,
                device_id={axis: peer_of(axis, offset)},
                device_id_type=pl.DeviceIdType.MESH,
            )
    pl.semaphore_wait(barrier, ka_size + pb_size - 2)

    def begin(axis, phase, source_of, target):
        size, send, recv = (
            (ka_size, ka_send, ka_recv) if axis == "ka" else (pb_size, pb_send, pb_recv)
        )
        copies = []
        for offset in range(1, size):
            peer = peer_of(axis, offset)
            copy = pltpu.make_async_remote_copy(
                src_ref=source_of(peer),
                dst_ref=target,
                send_sem=send.at[phase, offset],
                recv_sem=recv.at[phase, offset],
                device_id={axis: peer},
                device_id_type=pl.DeviceIdType.MESH,
            )
            copy.start()
            copies.append(copy)
        return copies

    def finish(copies):
        for copy in copies:
            copy.wait()

    def scattered_sum(axis, phase, value, tail, out, arrived, whole):
        me, size, share = (
            (ka_me, ka_size, ka_share) if axis == "ka" else (pb_me, pb_size, pb_share)
        )
        out[:, :share, :] = value.reshape(size, share, width)
        out[:, share:, :] = jnp.broadcast_to(tail[None], (size, 8, width))
        copies = begin(axis, phase, lambda peer: out.at[peer], arrived.at[me])
        arrived[me] = out[me]
        finish(copies)
        total = arrived[0]
        for source in range(1, size):
            total = total + arrived[source]
        whole[me] = total[:share]
        finish(begin(axis, phase + 1, lambda peer: whole.at[me], whole.at[me]))
        return whole[...].reshape(size * share, width), total[share:]

    def matmul(left_side, right_side):
        return jnp.dot(
            left_side, right_side, precision=highest, preferred_element_type=jnp.float32
        )

    def tail_rows(*rows):
        place = lax.broadcasted_iota(jnp.int32, (8, width), 0)
        tail = jnp.zeros((8, width), jnp.float32)
        for number, row in enumerate(rows):
            tail = jnp.where(place == number, row, tail)
        return tail

    copies = begin("ka", 0, lambda peer: part_ref.at[peer], stats_in.at[ka_me])
    stats_in[ka_me] = part_ref[ka_me]
    flipped[...] = kept_ref[...].T
    finish(copies)

    def column(source, number):
        return stats_in[source, :, width + number : width + number + 1]

    top = column(0, 0)
    kept_top = column(0, 2)
    for source in range(1, ka_size):
        top = jnp.maximum(top, column(source, 0))
        kept_top = jnp.maximum(kept_top, column(source, 2))
    total = jnp.zeros_like(top)
    kept_total = jnp.zeros_like(top)
    numerator = jnp.zeros((ka_share, width), jnp.float32)
    for source in range(ka_size):
        factor = jnp.exp(column(source, 0) - top)
        total = total + column(source, 1) * factor
        numerator = numerator + stats_in[source, :, :width] * factor
        kept_total = kept_total + column(source, 3) * jnp.exp(column(source, 2) - kept_top)
    lane = lax.broadcasted_iota(jnp.int32, (ka_share, width), 1)
    stats_all[ka_me, :, :width] = numerator / total
    stats_all[ka_me, :, width:] = jnp.where(lane == 0, kept_top, kept_total)
    finish(begin("ka", 1, lambda peer: stats_all.at[ka_me], stats_all.at[ka_me]))
    target = stats_all[:, :, :width].reshape(query_rows, width)
    joint_top = stats_all[:, :, width : width + 1].reshape(query_rows, 1)
    joint_total = stats_all[:, :, width + 1 : width + 2].reshape(query_rows, 1)
    own_top = part_ref[:, :, width + 2 : width + 3].reshape(query_rows, 1)
    scale = jnp.exp(own_top - joint_top) / joint_total

    no_tail = jnp.zeros((8, width), jnp.float32)
    residual, _ = scattered_sum(
        "pb",
        0,
        matmul(flipped[...], scale * target),
        no_tail,
        pb_out.at[0],
        pb_in.at[0],
        pb_all.at[0],
    )
    fitted = jnp.zeros_like(residual)
    direction = residual
    updates = None
    norm_now = None
    length_now = None
    for iteration in range(ITERS):
        forward = scale * matmul(kept_ref[...], residual)
        tail = tail_rows(column_sums(residual, residual), column_sums(residual, direction))
        summed, tail = scattered_sum(
            "ka",
            2 + 2 * iteration,
            forward,
            tail,
            ka_out.at[iteration],
            ka_in.at[iteration],
            ka_all.at[iteration],
        )
        norm_next = tail[0:1]
        if iteration == 0:
            updates = summed
            length_now = norm_next
        else:
            ratio = norm_next / norm_now
            direction = residual + ratio * direction
            updates = summed + ratio * updates
            length_now = norm_next + 2.0 * ratio * tail[1:2] + ratio * ratio * length_now
        norm_now = norm_next
        energy = tail_rows(column_sums(updates, updates))
        if iteration + 1 == ITERS:
            tail_out[...] = energy
            copies = begin("pb", 2 * ITERS, lambda peer: tail_out, tail_in.at[pb_me])
            tail_in[pb_me] = energy
            finish(copies)
            energy = tail_in[0]
            for source in range(1, pb_size):
                energy = energy + tail_in[source]
            step_length = norm_now / (energy[0:1] + ridge_weight * length_now)
            fitted_ref[...] = fitted + step_length * direction
        else:
            image, energy = scattered_sum(
                "pb",
                2 + 2 * iteration,
                matmul(flipped[...], scale * updates),
                energy,
                pb_out.at[iteration + 1],
                pb_in.at[iteration + 1],
                pb_all.at[iteration + 1],
            )
            step_length = norm_now / (energy[0:1] + ridge_weight * length_now)
            fitted = fitted + step_length * direction
            residual = residual - step_length * (image + ridge_weight * direction)


def fit(part, kept_exponent):
    ka_size, pb_size = lax.axis_size("ka"), lax.axis_size("pb")
    query_rows, kept_rows = kept_exponent.shape
    width = part.shape[1] // 2
    ka_share, pb_share = query_rows // ka_size, kept_rows // pb_size
    space = functools.partial(pltpu.VMEM, dtype=jnp.float32)
    return pl.pallas_call(
        functools.partial(fit_kernel, ka_size, pb_size),
        out_shape=jax.ShapeDtypeStruct((kept_rows, width), jnp.float32),
        in_specs=[pl.BlockSpec(memory_space=pltpu.VMEM)] * 2,
        out_specs=pl.BlockSpec(memory_space=pltpu.VMEM),
        scratch_shapes=[
            space((kept_rows, query_rows)),
            space((ka_size, ka_share, 2 * width)),
            space((ka_size, ka_share, 2 * width)),
            space((ITERS, ka_size, ka_share + 8, width)),
            space((ITERS, ka_size, ka_share + 8, width)),
            space((ITERS, ka_size, ka_share, width)),
            space((ITERS, pb_size, pb_share + 8, width)),
            space((ITERS, pb_size, pb_share + 8, width)),
            space((ITERS, pb_size, pb_share, width)),
            space((8, width)),
            space((pb_size, 8, width)),
            pltpu.SemaphoreType.DMA((2 + 2 * ITERS, ka_size)),
            pltpu.SemaphoreType.DMA((2 + 2 * ITERS, ka_size)),
            pltpu.SemaphoreType.DMA((2 * ITERS + 1, pb_size)),
            pltpu.SemaphoreType.DMA((2 * ITERS + 1, pb_size)),
        ],
        compiler_params=pltpu.CompilerParams(
            collective_id=0, has_side_effects=True, vmem_limit_bytes=40 * 1024 * 1024
        ),
    )(part.reshape(ka_size, ka_share, 2 * width), kept_exponent)


def thirds(value):
    first = value.astype(jnp.bfloat16)
    rest = value - first.astype(jnp.float32)
    second = rest.astype(jnp.bfloat16)
    third = (rest - second.astype(jnp.float32)).astype(jnp.bfloat16)
    return first, second, third


def target_kernel(inverse_root, queries_ref, keys_ref, values_ref, kept_ref, part_ref, wide, top, total, sums):
    width = queries_ref.shape[1]

    @pl.when(pl.program_id(0) == 0)
    def _():
        one, two, three = thirds(queries_ref[...])
        wide[...] = jnp.concatenate((one, one, two, one, three, two), axis=1)
        top[...] = jnp.full_like(top, -jnp.inf)
        total[...] = jnp.zeros_like(total)
        sums[...] = jnp.zeros_like(sums)

    one, two, three = thirds(keys_ref[...])
    scores = (
        lax.dot_general(
            wide[...],
            jnp.concatenate((one, two, one, three, one, two), axis=1),
            (((1,), (1,)), ((), ())),
            preferred_element_type=jnp.float32,
        )
        * inverse_root
    )
    top_next = jnp.maximum(top[...], jnp.max(scores, axis=1, keepdims=True))
    factor = jnp.exp(top[...] - top_next)
    exponent = jnp.exp(scores - top_next)
    top[...] = top_next
    total[...] = total[...] * factor + jnp.sum(exponent, axis=1, keepdims=True)
    one, two, three = thirds(values_ref[...])
    high, middle, low = thirds(exponent)
    pair = jnp.concatenate((one, two), axis=1)
    product = functools.partial(jnp.dot, preferred_element_type=jnp.float32)
    both = product(high, pair) + product(middle, pair)
    small = product(high, three) + product(low, one)
    sums[...] = sums[...] * factor + (both[:, :width] + (both[:, width:] + small))

    @pl.when(pl.program_id(0) == pl.num_programs(0) - 1)
    def _():
        lane = lax.broadcasted_iota(jnp.int32, kept_ref.shape, 1)
        stats = jnp.where(lane == 0, top[...], jnp.where(lane == 1, total[...], kept_ref[...]))
        part_ref[:, :width] = sums[...]
        part_ref[:, width:] = stats


def target_part(queries, cache_keys, cache_values, kept_stats, inverse_root):
    query_rows, width = queries.shape
    block_size = min(2048, cache_keys.shape[0])
    fixed = pl.BlockSpec((query_rows, width), lambda block: (0, 0))
    moving = pl.BlockSpec((block_size, width), lambda block: (block, 0))
    return pl.pallas_call(
        functools.partial(target_kernel, inverse_root),
        grid=(cache_keys.shape[0] // block_size,),
        out_shape=jax.ShapeDtypeStruct((query_rows, 2 * width), jnp.float32),
        in_specs=[fixed, moving, moving, fixed],
        out_specs=pl.BlockSpec((query_rows, 2 * width), lambda block: (0, 0)),
        scratch_shapes=[
            pltpu.VMEM((query_rows, 6 * width), jnp.bfloat16),
            pltpu.VMEM((query_rows, 1), jnp.float32),
            pltpu.VMEM((query_rows, 1), jnp.float32),
            pltpu.VMEM((query_rows, width), jnp.float32),
        ],
        compiler_params=pltpu.CompilerParams(vmem_limit_bytes=40 * 1024 * 1024),
    )(queries, cache_keys, cache_values, kept_stats)


def halves(value):
    first = value.astype(jnp.bfloat16)
    return first, (value - first.astype(jnp.float32)).astype(jnp.bfloat16)


def product(left_side, right_side, left_dim=1, right_dim=0):
    return lax.dot_general(
        left_side,
        right_side,
        (((left_dim,), (right_dim,)), ((), ())),
        preferred_element_type=jnp.float32,
    )


def wide_queries(value):
    one, two, three = thirds(value)
    return jnp.concatenate((one, one, two, one, three, two), axis=1)


def wide_keys(value):
    one, two, three = thirds(value)
    return jnp.concatenate((one, two, one, three, one, two), axis=1)


def stacked(value):
    return jnp.concatenate(thirds(value), axis=0)


def folded(value):
    rows = value.shape[0] // 3
    return value[:rows] + (value[rows : 2 * rows] + value[2 * rows :])


def order_of(size):
    return sorted(range(1, size), key=lambda offset: abs(2 * offset - size))


def whole_kernel(
    ka_size,
    pb_size,
    exponent_scale,
    index_ref,
    queries_hbm,
    keys_hbm,
    values_hbm,
    fitted_ref,
    keys_v,
    values_v,
    sums,
    queries_all,
    queries_wide,
    kept_all,
    part,
    part_in,
    stats,
    stats_in,
    first_part,
    second_part,
    first_turned,
    second_turned,
    kept_stats,
    scale,
    target_all,
    residual_v,
    half_out,
    core_in,
    side_out,
    side_in,
    updates_all,
    energy_out,
    energy_in,
    piece_out,
    piece_in,
    blocks_all,
    factors,
    load_sems,
    ka_send,
    ka_recv,
    pb_send,
    pb_recv,
    pair_send,
    pair_recv,
):
    ka_me = lax.axis_index("ka")
    pb_me = lax.axis_index("pb")
    query_rows, width = queries_hbm.shape
    columns = width // ka_size
    pieces = query_rows // 128
    group = kept_all.shape[1]
    cache_rows = keys_hbm.shape[0]
    block = cache_rows // pb_size
    stride = block // group
    core_bit = lax.rem(pb_me, 2)
    core_peer = pb_me + 1 - 2 * core_bit
    side_peer = lax.rem(pb_me + 2, 4)

    def peer_of(axis, offset):
        if axis == "ka":
            return lax.rem(ka_me + offset, ka_size)
        return lax.rem(pb_me + offset, pb_size)

    barrier = pltpu.get_barrier_semaphore()
    for axis, size in (("ka", ka_size), ("pb", pb_size)):
        for offset in range(1, size):
            pl.semaphore_signal(
                barrier,
                inc=1,
                device_id={axis: peer_of(axis, offset)},
                device_id_type=pl.DeviceIdType.MESH,
            )

    def begin(axis, phase, source_of, target):
        size, send, recv = (
            (ka_size, ka_send, ka_recv) if axis == "ka" else (pb_size, pb_send, pb_recv)
        )
        copies = []
        for offset in order_of(size):
            peer = peer_of(axis, offset)
            copy = pltpu.make_async_remote_copy(
                src_ref=source_of(peer),
                dst_ref=target,
                send_sem=send.at[phase, offset],
                recv_sem=recv.at[phase, offset],
                device_id={axis: peer},
                device_id_type=pl.DeviceIdType.MESH,
            )
            copy.start()
            copies.append(copy)
        return copies

    def pair(phase, peer, source, target):
        copy = pltpu.make_async_remote_copy(
            src_ref=source,
            dst_ref=target,
            send_sem=pair_send.at[phase],
            recv_sem=pair_recv.at[phase],
            device_id={"pb": peer},
            device_id_type=pl.DeviceIdType.MESH,
        )
        copy.start()
        return copy

    def finish(copies):
        for copy in copies:
            copy.wait()

    def load(number, keys):
        source = pl.ds(pl.multiple_of(lax.rem(pb_me + number, pb_size) * block, block), block)
        hbm, vmem, kind = (keys_hbm, keys_v, 0) if keys else (values_hbm, values_v, 1)
        return pltpu.make_async_copy(
            hbm.at[source], vmem.at[number], load_sems.at[kind, number]
        )

    query_load = pltpu.make_async_copy(
        queries_hbm, queries_all.at[pb_me], load_sems.at[2, 0]
    )
    load(0, True).start()
    query_load.start()
    for number in range(pb_size):
        if number > 0:
            load(number, True).start()
        load(number, False).start()

    def pack(target, top, total):
        for piece in range(pieces):
            lanes = slice(piece * 128, (piece + 1) * 128)
            target[piece : piece + 1, :] = top[:, lanes]
            target[pieces + piece : pieces + piece + 1, :] = total[:, lanes]

    def unpack(value):
        return jnp.concatenate([value[piece : piece + 1] for piece in range(pieces)], axis=1)

    load(0, True).wait()
    place = index_ref[pl.ds(pb_me, 1), :] - (ka_me * cache_rows + pb_me * block)
    place = jnp.broadcast_to(place.astype(jnp.float32), (group, group)).T
    first_row = lax.broadcasted_iota(jnp.int32, (group, group), 0) * stride
    offset_row = place - first_row.astype(jnp.float32)
    kept = jnp.zeros((group, width), jnp.float32)
    for step in range(stride):
        kept = jnp.where(
            offset_row == float(step), keys_v[0, pl.ds(step, group, stride=stride), :], kept
        )
    kept_all[ka_me] = kept

    pl.semaphore_wait(barrier, ka_size + pb_size - 2)
    kept_copies = begin("ka", 0, lambda peer: kept_all.at[ka_me], kept_all.at[ka_me])
    query_load.wait()
    query_copies = begin("pb", 0, lambda peer: queries_all.at[pb_me], queries_all.at[pb_me])

    own_wide = wide_queries(queries_all[pb_me] * exponent_scale)

    def target_block(number, carry):
        if carry is None:
            scores = product(wide_keys(keys_v[number]), own_wide, 1, 1)
            top_next = jnp.max(scores, axis=0, keepdims=True)
        else:
            load(number, True).wait()
            scores = product(wide_keys(keys_v[number]), own_wide, 1, 1)
            top, total = carry
            top_next = jnp.maximum(top, jnp.max(scores, axis=0, keepdims=True))
            factor = jnp.exp2(top - top_next)
        load(number, False).wait()
        turned = jnp.concatenate(halves(values_v[number].T), axis=0)
        exponent = jnp.exp2(scores - top_next)
        block_total = jnp.sum(exponent, axis=0, keepdims=True)
        added = product(
            jnp.concatenate((turned, turned), axis=1),
            jnp.concatenate(halves(exponent), axis=0),
        )
        if carry is None:
            sums[...] = added
            return top_next, block_total
        sums[...] = sums[...] * factor + added
        return top_next, total * factor + block_total

    top, total = lax.fori_loop(1, pb_size, target_block, target_block(0, None))
    part[...] = (sums[:width] + sums[width:]).reshape(ka_size, columns, query_rows)
    pack(stats, top, total)
    stats_copies = begin("ka", 2, lambda peer: stats, stats_in.at[ka_me])
    part_copies = begin("ka", 1, lambda peer: part.at[peer], part_in.at[ka_me])
    part_copies = list(zip(order_of(ka_size), part_copies))
    part_in[ka_me] = part[ka_me]
    stats_in[ka_me] = stats[...]

    finish(query_copies)
    finish(kept_copies)
    kept_wide = wide_keys(kept_all[...].reshape(ka_size * group, width))

    @pl.loop(0, pb_size)
    def _(number):
        queries_wide[...] = wide_queries(queries_all[number] * exponent_scale)
        scores = product(kept_wide, queries_wide[...], 1, 1)
        top = jnp.max(scores, axis=0, keepdims=True)
        exponent = jnp.exp2(scores - top)
        pack(kept_stats.at[pb_me, number], top, jnp.sum(exponent, axis=0, keepdims=True))
        one, two = halves(exponent)
        first_part[number] = one
        second_part[number] = two
        first_turned[number] = one.T
        second_turned[number] = two.T

    kept_stats_copies = begin("pb", 1, lambda peer: kept_stats.at[pb_me], kept_stats.at[pb_me])

    finish(stats_copies)
    joint_top = stats_in[0, :pieces]
    for source in range(1, ka_size):
        joint_top = jnp.maximum(joint_top, stats_in[source, :pieces])
    joint_total = jnp.zeros_like(joint_top)
    for source in range(ka_size):
        joint_total = joint_total + stats_in[source, pieces:] * jnp.exp2(
            stats_in[source, :pieces] - joint_top
        )

    def weighted(source):
        return part_in[source] * unpack(jnp.exp2(stats_in[source, :pieces] - joint_top))

    numerator = weighted(ka_me)
    for offset, copy in part_copies:
        copy.wait()
        numerator = numerator + weighted(lax.rem(ka_me + ka_size - offset, ka_size))
    target_all[pb_me] = numerator / unpack(joint_total)
    target_copies = begin("pb", 2, lambda peer: target_all.at[pb_me], target_all.at[pb_me])

    finish(kept_stats_copies)
    for number in range(pb_size):
        joint_top = kept_stats[0, number, :pieces]
        for source in range(1, pb_size):
            joint_top = jnp.maximum(joint_top, kept_stats[source, number, :pieces])
        joint_total = jnp.zeros_like(joint_top)
        for source in range(pb_size):
            joint_total = joint_total + kept_stats[source, number, pieces:] * jnp.exp2(
                kept_stats[source, number, :pieces] - joint_top
            )
        own_top = kept_stats[pb_me, number, :pieces]
        scale[number] = jnp.broadcast_to(
            unpack(jnp.exp2(own_top - joint_top) / joint_total), (columns, query_rows)
        )

    def backward(number, vector):
        rows = stacked(scale[number] * vector)
        return product(rows, first_turned[number]) + product(rows, second_turned[number])

    lane = lax.broadcasted_iota(jnp.int32, (columns, 128), 1)

    def lane_sums(value):
        return jnp.sum(value, axis=1, keepdims=True)

    def long(number):
        return query_rows + 128 if number == 0 else query_rows

    def forward(phase, slot, vector, tail):
        rows = stacked(vector)

        def chunk_of(half, number):
            chunk = 2 * half + number
            term = folded(product(rows, first_part[chunk]) + product(rows, second_part[chunk]))
            half_out[slot, half, number, :, :query_rows] = scale[chunk] * term
            if number == 0:
                half_out[slot, half, number, :, query_rows:] = tail

        core_copies = []
        for number in range(2):
            chunk_of(1 - core_bit, number)
            lanes = pl.ds(0, long(number))
            core_copies.append(
                pair(
                    phase + number,
                    core_peer,
                    half_out.at[slot, 1 - core_bit, number, :, lanes],
                    core_in.at[slot, number, :, lanes],
                )
            )
        side_copies = []
        for number in range(2):
            chunk_of(core_bit, number)
            core_copies[number].wait()
            lanes = pl.ds(0, long(number))
            side_out[slot, number, :, lanes] = (
                half_out[slot, core_bit, number, :, lanes] + core_in[slot, number, :, lanes]
            )
            side_copies.append(
                pair(
                    phase + 2 + number,
                    side_peer,
                    side_out.at[slot, number, :, lanes],
                    side_in.at[slot, number, :, lanes],
                )
            )
        return side_copies

    def spread(phase, slot, value):
        for target in range(ka_size):
            piece_out[slot, target] = value[:, target * group : (target + 1) * group]
        piece_in[slot, ka_me] = piece_out[slot, ka_me]
        return begin(
            "ka", phase, lambda peer: piece_out.at[slot, peer], piece_in.at[slot, ka_me]
        )

    def share(phase, slot):
        blocks_all[slot, pb_me] = piece_in[slot].reshape(width, group)
        return begin(
            "pb", phase, lambda peer: blocks_all.at[slot, pb_me], blocks_all.at[slot, pb_me]
        )

    image = backward(pb_me, target_all[pb_me])
    for offset, copy in sorted(
        zip(order_of(pb_size), target_copies), key=lambda item: item[0] % 2, reverse=True
    ):
        copy.wait()
        source = lax.rem(pb_me + pb_size - offset, pb_size)
        image = image + backward(source, target_all[source])
    residual = folded(image)
    residual_v[...] = residual
    side_copies = forward(
        0, 0, residual, jnp.where(lane == 0, lane_sums(residual * residual), 0.0)
    )
    spread_copies = spread(3, 0, residual)
    update_copies = []
    for number in range(2):
        side_copies[number].wait()
        joined = side_out[0, number, :, :query_rows] + side_in[0, number, :, :query_rows]
        updates_all[2 * core_bit + number] = joined
        update_copies.append(
            pair(
                4 + number,
                core_peer,
                updates_all.at[2 * core_bit + number],
                updates_all.at[2 * core_bit + number],
            )
        )
    norm_first = (side_out[0, 0, :, query_rows:] + side_in[0, 0, :, query_rows:])[:, :1]
    image = None
    energy = None
    for half in (core_bit, 1 - core_bit):
        for number in range(2):
            if half is not core_bit:
                update_copies[number].wait()
            updates = updates_all[2 * half + number]
            term = backward(2 * half + number, updates)
            image = term if image is None else image + term
            term = lane_sums(updates * updates)
            energy = term if energy is None else energy + term
        if half is core_bit:
            finish(spread_copies)
            first_copies = share(3, 0)
    step_first = norm_first / (energy + ridge_weight * norm_first)
    residual = residual_v[...]
    after = residual - step_first * (folded(image) + ridge_weight * residual)
    spread_copies = spread(4, 1, after)
    tail = jnp.where(
        lane == 0,
        lane_sums(after * after),
        jnp.where(lane == 1, lane_sums(after * residual), 0.0),
    )
    side_copies = forward(6, 1, after, tail)
    finish(side_copies)
    tail = side_out[1, 0, :, query_rows:] + side_in[1, 0, :, query_rows:]
    norm_second = tail[:, :1]
    ratio = norm_second / norm_first
    energy = None
    for number in range(2):
        updates = side_out[1, number, :, :query_rows] + side_in[1, number, :, :query_rows]
        updates = updates + ratio * updates_all[2 * core_bit + number]
        term = lane_sums(updates * updates)
        energy = term if energy is None else energy + term
    energy_out[...] = jnp.broadcast_to(energy, energy_out.shape)
    energy_copy = pair(10, core_peer, energy_out, energy_in)
    finish(spread_copies)
    second_copies = share(4, 1)
    energy_copy.wait()
    energy = energy_out[:, :1] + energy_in[:, :1]
    length = norm_second + 2.0 * ratio * tail[:, 1:2] + ratio * ratio * norm_first
    step_second = norm_second / (energy + ridge_weight * length)
    factors[ka_me] = jnp.where(lane == 0, step_first + step_second * ratio, step_second)
    factor_copies = begin("ka", 5, lambda peer: factors.at[ka_me], factors.at[ka_me])
    finish(first_copies)
    finish(second_copies)
    turned = [[blocks_all[slot, number].T for number in range(pb_size)] for slot in range(2)]
    finish(factor_copies)
    both = factors[...].reshape(width, 128).T
    for number in range(pb_size):
        fitted_ref[number * group : (number + 1) * group, :] = (
            both[0:1] * turned[0][number] + both[1:2] * turned[1][number]
        )


def whole(queries, cache_keys, cache_values, kept_index, exponent_scale):
    ka_size, pb_size = lax.axis_size("ka"), lax.axis_size("pb")
    query_rows, width = queries.shape
    kept_rows = kept_index.shape[0]
    cache_rows = cache_keys.shape[0]
    group, block, columns = kept_rows // pb_size, cache_rows // pb_size, width // ka_size
    pieces = query_rows // 128
    joint = ka_size * group
    space = functools.partial(pltpu.VMEM, dtype=jnp.float32)
    narrow = functools.partial(pltpu.VMEM, dtype=jnp.bfloat16)
    return pl.pallas_call(
        functools.partial(whole_kernel, ka_size, pb_size, exponent_scale),
        out_shape=jax.ShapeDtypeStruct((kept_rows, width), jnp.float32),
        in_specs=[pl.BlockSpec(memory_space=pltpu.VMEM)]
        + [pl.BlockSpec(memory_space=pl.ANY)] * 3,
        out_specs=pl.BlockSpec(memory_space=pltpu.VMEM),
        scratch_shapes=[
            space((pb_size, block, width)),
            space((pb_size, block, width)),
            space((2 * width, query_rows)),
            space((pb_size, query_rows, width)),
            narrow((query_rows, 6 * width)),
            space((ka_size, group, width)),
            space((ka_size, columns, query_rows)),
            space((ka_size, columns, query_rows)),
            space((2 * pieces, 128)),
            space((ka_size, 2 * pieces, 128)),
            narrow((pb_size, joint, query_rows)),
            narrow((pb_size, joint, query_rows)),
            narrow((pb_size, query_rows, joint)),
            narrow((pb_size, query_rows, joint)),
            space((pb_size, pb_size, 2 * pieces, 128)),
            space((pb_size, columns, query_rows)),
            space((pb_size, columns, query_rows)),
            space((columns, joint)),
            space((2, 2, 2, columns, query_rows + 128)),
            space((2, 2, columns, query_rows + 128)),
            space((2, 2, columns, query_rows + 128)),
            space((2, 2, columns, query_rows + 128)),
            space((pb_size, columns, query_rows)),
            space((columns, 128)),
            space((columns, 128)),
            space((2, ka_size, columns, group)),
            space((2, ka_size, columns, group)),
            space((2, pb_size, width, group)),
            space((ka_size, columns, 128)),
            pltpu.SemaphoreType.DMA((3, pb_size)),
            pltpu.SemaphoreType.DMA((6, ka_size)),
            pltpu.SemaphoreType.DMA((6, ka_size)),
            pltpu.SemaphoreType.DMA((5, pb_size)),
            pltpu.SemaphoreType.DMA((5, pb_size)),
            pltpu.SemaphoreType.DMA((11,)),
            pltpu.SemaphoreType.DMA((11,)),
        ],
        compiler_params=pltpu.CompilerParams(
            collective_id=1, has_side_effects=True, vmem_limit_bytes=107 * 512 * 1024
        ),
    )(kept_index.reshape(pb_size, group), queries, cache_keys, cache_values)


def suits(ka_size, pb_size, queries, cache_keys, kept_index):
    width = queries.shape[1]
    group = kept_index.shape[0] // pb_size
    return (
        pb_size == 4
        and width == 128
        and group == 128
        and queries.shape[0] == 512
        and cache_keys.shape[0] == 8192
        and width % (8 * ka_size) == 0
    )


def shards(queries, cache_keys, cache_values, kept_index):
    head_width = queries.shape[1]
    inverse_root = 1.0 / math.sqrt(head_width)
    cache_rows = cache_keys.shape[0]
    if suits(lax.axis_size("ka"), lax.axis_size("pb"), queries, cache_keys, kept_index):
        exponent_scale = inverse_root * math.log2(math.e)
        return whole(queries, cache_keys, cache_values, kept_index, exponent_scale)

    local_kept = kept_index - lax.axis_index("ka") * cache_rows
    kept_keys = jnp.take(cache_keys, local_kept, axis=0)
    kept_scores = contract(queries, kept_keys, 1, 1) * inverse_root
    kept_top = jnp.max(kept_scores, axis=1)
    kept_exponent = jnp.exp(kept_scores - kept_top[:, None])
    kept_total = jnp.sum(kept_exponent, axis=1)

    zero = jnp.zeros_like(kept_top)
    stats = jnp.stack((zero, zero, kept_top, kept_total), axis=1)
    stats = jnp.pad(stats, ((0, 0), (0, head_width - 4)))
    return fit(
        target_part(queries, cache_keys, cache_values, stats, inverse_root), kept_exponent
    )


def solution(mesh):
    in_specs = (P("pb", None), P("ka", None), P("ka", None), P("ka"))
    out_specs = P("ka", None)
    return jax.shard_map(shards, mesh=mesh, in_specs=in_specs, out_specs=out_specs, check_vma=False)
```

```python
import functools
import math

import jax
import jax.numpy as jnp
from jax import lax
from jax.experimental import pallas as pl
from jax.experimental.pallas import tpu as pltpu
from jax.sharding import PartitionSpec as P

ITERS = 2


ridge_weight = 0.01
highest = lax.Precision.HIGHEST


def contract(left_side, right_side, left_dim, right_dim):
    return lax.dot_general(
        left_side,
        right_side,
        (((left_dim,), (right_dim,)), ((), ())),
        precision=highest,
        preferred_element_type=jnp.float32,
    )


def column_sums(left_side, right_side):
    return jnp.sum(left_side * right_side, axis=0, keepdims=True)


def fit_kernel(
    ka_size,
    pb_size,
    part_ref,
    kept_ref,
    fitted_ref,
    flipped,
    stats_in,
    stats_all,
    ka_out,
    ka_in,
    ka_all,
    pb_out,
    pb_in,
    pb_all,
    tail_out,
    tail_in,
    ka_send,
    ka_recv,
    pb_send,
    pb_recv,
):
    ka_me = lax.axis_index("ka")
    pb_me = lax.axis_index("pb")
    width = fitted_ref.shape[1]
    query_rows = kept_ref.shape[0]
    kept_rows = kept_ref.shape[1]
    ka_share = query_rows // ka_size
    pb_share = kept_rows // pb_size

    def peer_of(axis, offset):
        size = ka_size if axis == "ka" else pb_size
        me = ka_me if axis == "ka" else pb_me
        return lax.rem(me + offset, size)

    barrier = pltpu.get_barrier_semaphore()
    for axis, size in (("ka", ka_size), ("pb", pb_size)):
        for offset in range(1, size):
            pl.semaphore_signal(
                barrier,
                inc=1,
                device_id={axis: peer_of(axis, offset)},
                device_id_type=pl.DeviceIdType.MESH,
            )
    pl.semaphore_wait(barrier, ka_size + pb_size - 2)

    def begin(axis, phase, source_of, target):
        size, send, recv = (
            (ka_size, ka_send, ka_recv) if axis == "ka" else (pb_size, pb_send, pb_recv)
        )
        copies = []
        for offset in range(1, size):
            peer = peer_of(axis, offset)
            copy = pltpu.make_async_remote_copy(
                src_ref=source_of(peer),
                dst_ref=target,
                send_sem=send.at[phase, offset],
                recv_sem=recv.at[phase, offset],
                device_id={axis: peer},
                device_id_type=pl.DeviceIdType.MESH,
            )
            copy.start()
            copies.append(copy)
        return copies

    def finish(copies):
        for copy in copies:
            copy.wait()

    def scattered_sum(axis, phase, value, tail, out, arrived, whole):
        me, size, share = (
            (ka_me, ka_size, ka_share) if axis == "ka" else (pb_me, pb_size, pb_share)
        )
        out[:, :share, :] = value.reshape(size, share, width)
        out[:, share:, :] = jnp.broadcast_to(tail[None], (size, 8, width))
        copies = begin(axis, phase, lambda peer: out.at[peer], arrived.at[me])
        arrived[me] = out[me]
        finish(copies)
        total = arrived[0]
        for source in range(1, size):
            total = total + arrived[source]
        whole[me] = total[:share]
        finish(begin(axis, phase + 1, lambda peer: whole.at[me], whole.at[me]))
        return whole[...].reshape(size * share, width), total[share:]

    def matmul(left_side, right_side):
        return jnp.dot(
            left_side, right_side, precision=highest, preferred_element_type=jnp.float32
        )

    def tail_rows(*rows):
        place = lax.broadcasted_iota(jnp.int32, (8, width), 0)
        tail = jnp.zeros((8, width), jnp.float32)
        for number, row in enumerate(rows):
            tail = jnp.where(place == number, row, tail)
        return tail

    copies = begin("ka", 0, lambda peer: part_ref.at[peer], stats_in.at[ka_me])
    stats_in[ka_me] = part_ref[ka_me]
    flipped[...] = kept_ref[...].T
    finish(copies)

    def column(source, number):
        return stats_in[source, :, width + number : width + number + 1]

    top = column(0, 0)
    kept_top = column(0, 2)
    for source in range(1, ka_size):
        top = jnp.maximum(top, column(source, 0))
        kept_top = jnp.maximum(kept_top, column(source, 2))
    total = jnp.zeros_like(top)
    kept_total = jnp.zeros_like(top)
    numerator = jnp.zeros((ka_share, width), jnp.float32)
    for source in range(ka_size):
        factor = jnp.exp(column(source, 0) - top)
        total = total + column(source, 1) * factor
        numerator = numerator + stats_in[source, :, :width] * factor
        kept_total = kept_total + column(source, 3) * jnp.exp(column(source, 2) - kept_top)
    lane = lax.broadcasted_iota(jnp.int32, (ka_share, width), 1)
    stats_all[ka_me, :, :width] = numerator / total
    stats_all[ka_me, :, width:] = jnp.where(lane == 0, kept_top, kept_total)
    finish(begin("ka", 1, lambda peer: stats_all.at[ka_me], stats_all.at[ka_me]))
    target = stats_all[:, :, :width].reshape(query_rows, width)
    joint_top = stats_all[:, :, width : width + 1].reshape(query_rows, 1)
    joint_total = stats_all[:, :, width + 1 : width + 2].reshape(query_rows, 1)
    own_top = part_ref[:, :, width + 2 : width + 3].reshape(query_rows, 1)
    scale = jnp.exp(own_top - joint_top) / joint_total

    no_tail = jnp.zeros((8, width), jnp.float32)
    residual, _ = scattered_sum(
        "pb",
        0,
        matmul(flipped[...], scale * target),
        no_tail,
        pb_out.at[0],
        pb_in.at[0],
        pb_all.at[0],
    )
    fitted = jnp.zeros_like(residual)
    direction = residual
    updates = None
    norm_now = None
    length_now = None
    for iteration in range(ITERS):
        forward = scale * matmul(kept_ref[...], residual)
        tail = tail_rows(column_sums(residual, residual), column_sums(residual, direction))
        summed, tail = scattered_sum(
            "ka",
            2 + 2 * iteration,
            forward,
            tail,
            ka_out.at[iteration],
            ka_in.at[iteration],
            ka_all.at[iteration],
        )
        norm_next = tail[0:1]
        if iteration == 0:
            updates = summed
            length_now = norm_next
        else:
            ratio = norm_next / norm_now
            direction = residual + ratio * direction
            updates = summed + ratio * updates
            length_now = norm_next + 2.0 * ratio * tail[1:2] + ratio * ratio * length_now
        norm_now = norm_next
        energy = tail_rows(column_sums(updates, updates))
        if iteration + 1 == ITERS:
            tail_out[...] = energy
            copies = begin("pb", 2 * ITERS, lambda peer: tail_out, tail_in.at[pb_me])
            tail_in[pb_me] = energy
            finish(copies)
            energy = tail_in[0]
            for source in range(1, pb_size):
                energy = energy + tail_in[source]
            step_length = norm_now / (energy[0:1] + ridge_weight * length_now)
            fitted_ref[...] = fitted + step_length * direction
        else:
            image, energy = scattered_sum(
                "pb",
                2 + 2 * iteration,
                matmul(flipped[...], scale * updates),
                energy,
                pb_out.at[iteration + 1],
                pb_in.at[iteration + 1],
                pb_all.at[iteration + 1],
            )
            step_length = norm_now / (energy[0:1] + ridge_weight * length_now)
            fitted = fitted + step_length * direction
            residual = residual - step_length * (image + ridge_weight * direction)


def fit(part, kept_exponent):
    ka_size, pb_size = lax.axis_size("ka"), lax.axis_size("pb")
    query_rows, kept_rows = kept_exponent.shape
    width = part.shape[1] // 2
    ka_share, pb_share = query_rows // ka_size, kept_rows // pb_size
    space = functools.partial(pltpu.VMEM, dtype=jnp.float32)
    return pl.pallas_call(
        functools.partial(fit_kernel, ka_size, pb_size),
        out_shape=jax.ShapeDtypeStruct((kept_rows, width), jnp.float32),
        in_specs=[pl.BlockSpec(memory_space=pltpu.VMEM)] * 2,
        out_specs=pl.BlockSpec(memory_space=pltpu.VMEM),
        scratch_shapes=[
            space((kept_rows, query_rows)),
            space((ka_size, ka_share, 2 * width)),
            space((ka_size, ka_share, 2 * width)),
            space((ITERS, ka_size, ka_share + 8, width)),
            space((ITERS, ka_size, ka_share + 8, width)),
            space((ITERS, ka_size, ka_share, width)),
            space((ITERS, pb_size, pb_share + 8, width)),
            space((ITERS, pb_size, pb_share + 8, width)),
            space((ITERS, pb_size, pb_share, width)),
            space((8, width)),
            space((pb_size, 8, width)),
            pltpu.SemaphoreType.DMA((2 + 2 * ITERS, ka_size)),
            pltpu.SemaphoreType.DMA((2 + 2 * ITERS, ka_size)),
            pltpu.SemaphoreType.DMA((2 * ITERS + 1, pb_size)),
            pltpu.SemaphoreType.DMA((2 * ITERS + 1, pb_size)),
        ],
        compiler_params=pltpu.CompilerParams(
            collective_id=0, has_side_effects=True, vmem_limit_bytes=40 * 1024 * 1024
        ),
    )(part.reshape(ka_size, ka_share, 2 * width), kept_exponent)


def thirds(value):
    first = value.astype(jnp.bfloat16)
    rest = value - first.astype(jnp.float32)
    second = rest.astype(jnp.bfloat16)
    third = (rest - second.astype(jnp.float32)).astype(jnp.bfloat16)
    return first, second, third


def target_kernel(inverse_root, queries_ref, keys_ref, values_ref, kept_ref, part_ref, wide, top, total, sums):
    width = queries_ref.shape[1]

    @pl.when(pl.program_id(0) == 0)
    def _():
        one, two, three = thirds(queries_ref[...])
        wide[...] = jnp.concatenate((one, one, two, one, three, two), axis=1)
        top[...] = jnp.full_like(top, -jnp.inf)
        total[...] = jnp.zeros_like(total)
        sums[...] = jnp.zeros_like(sums)

    one, two, three = thirds(keys_ref[...])
    scores = (
        lax.dot_general(
            wide[...],
            jnp.concatenate((one, two, one, three, one, two), axis=1),
            (((1,), (1,)), ((), ())),
            preferred_element_type=jnp.float32,
        )
        * inverse_root
    )
    top_next = jnp.maximum(top[...], jnp.max(scores, axis=1, keepdims=True))
    factor = jnp.exp(top[...] - top_next)
    exponent = jnp.exp(scores - top_next)
    top[...] = top_next
    total[...] = total[...] * factor + jnp.sum(exponent, axis=1, keepdims=True)
    one, two, three = thirds(values_ref[...])
    high, middle, low = thirds(exponent)
    pair = jnp.concatenate((one, two), axis=1)
    product = functools.partial(jnp.dot, preferred_element_type=jnp.float32)
    both = product(high, pair) + product(middle, pair)
    small = product(high, three) + product(low, one)
    sums[...] = sums[...] * factor + (both[:, :width] + (both[:, width:] + small))

    @pl.when(pl.program_id(0) == pl.num_programs(0) - 1)
    def _():
        lane = lax.broadcasted_iota(jnp.int32, kept_ref.shape, 1)
        stats = jnp.where(lane == 0, top[...], jnp.where(lane == 1, total[...], kept_ref[...]))
        part_ref[:, :width] = sums[...]
        part_ref[:, width:] = stats


def target_part(queries, cache_keys, cache_values, kept_stats, inverse_root):
    query_rows, width = queries.shape
    block_size = min(2048, cache_keys.shape[0])
    fixed = pl.BlockSpec((query_rows, width), lambda block: (0, 0))
    moving = pl.BlockSpec((block_size, width), lambda block: (block, 0))
    return pl.pallas_call(
        functools.partial(target_kernel, inverse_root),
        grid=(cache_keys.shape[0] // block_size,),
        out_shape=jax.ShapeDtypeStruct((query_rows, 2 * width), jnp.float32),
        in_specs=[fixed, moving, moving, fixed],
        out_specs=pl.BlockSpec((query_rows, 2 * width), lambda block: (0, 0)),
        scratch_shapes=[
            pltpu.VMEM((query_rows, 6 * width), jnp.bfloat16),
            pltpu.VMEM((query_rows, 1), jnp.float32),
            pltpu.VMEM((query_rows, 1), jnp.float32),
            pltpu.VMEM((query_rows, width), jnp.float32),
        ],
        compiler_params=pltpu.CompilerParams(vmem_limit_bytes=40 * 1024 * 1024),
    )(queries, cache_keys, cache_values, kept_stats)


def halves(value):
    first = value.astype(jnp.bfloat16)
    return first, (value - first.astype(jnp.float32)).astype(jnp.bfloat16)


def product(left_side, right_side, left_dim=1, right_dim=0):
    return lax.dot_general(
        left_side,
        right_side,
        (((left_dim,), (right_dim,)), ((), ())),
        preferred_element_type=jnp.float32,
    )


def wide_queries(value):
    one, two, three = thirds(value)
    return jnp.concatenate((one, one, two, one, three, two), axis=1)


def wide_keys(value):
    one, two, three = thirds(value)
    return jnp.concatenate((one, two, one, three, one, two), axis=1)


def stacked(value):
    return jnp.concatenate(thirds(value), axis=0)


def folded(value):
    rows = value.shape[0] // 3
    return value[:rows] + (value[rows : 2 * rows] + value[2 * rows :])


def order_of(size):
    return sorted(range(1, size), key=lambda offset: abs(2 * offset - size))


def whole_kernel(
    ka_size,
    pb_size,
    exponent_scale,
    index_ref,
    queries_hbm,
    keys_hbm,
    values_hbm,
    fitted_ref,
    keys_v,
    values_v,
    sums,
    queries_all,
    queries_wide,
    kept_all,
    part,
    part_in,
    stats,
    stats_in,
    first_part,
    second_part,
    first_turned,
    second_turned,
    kept_stats,
    scale,
    target_all,
    residual_v,
    half_out,
    core_in,
    side_out,
    side_in,
    updates_all,
    energy_out,
    energy_in,
    piece_out,
    piece_in,
    blocks_all,
    factor_place,
    factors,
    load_sems,
    ka_send,
    ka_recv,
    pb_send,
    pb_recv,
    pair_send,
    pair_recv,
):
    ka_me = lax.axis_index("ka")
    pb_me = lax.axis_index("pb")
    query_rows, width = queries_hbm.shape
    columns = width // ka_size
    pieces = query_rows // 128
    group = kept_all.shape[1]
    cache_rows = keys_hbm.shape[0]
    block = cache_rows // pb_size
    stride = block // group
    core_bit = lax.rem(pb_me, 2)
    core_peer = pb_me + 1 - 2 * core_bit
    side_peer = lax.rem(pb_me + 2, 4)

    def peer_of(axis, offset):
        if axis == "ka":
            return lax.rem(ka_me + offset, ka_size)
        return lax.rem(pb_me + offset, pb_size)

    barrier = pltpu.get_barrier_semaphore()
    for axis, size in (("ka", ka_size), ("pb", pb_size)):
        for offset in range(1, size):
            pl.semaphore_signal(
                barrier,
                inc=1,
                device_id={axis: peer_of(axis, offset)},
                device_id_type=pl.DeviceIdType.MESH,
            )

    def begin(axis, phase, source_of, target):
        size, send, recv = (
            (ka_size, ka_send, ka_recv) if axis == "ka" else (pb_size, pb_send, pb_recv)
        )
        copies = []
        for offset in order_of(size):
            peer = peer_of(axis, offset)
            copy = pltpu.make_async_remote_copy(
                src_ref=source_of(peer),
                dst_ref=target,
                send_sem=send.at[phase, offset],
                recv_sem=recv.at[phase, offset],
                device_id={axis: peer},
                device_id_type=pl.DeviceIdType.MESH,
            )
            copy.start()
            copies.append(copy)
        return copies

    def pair(phase, peer, source, target):
        copy = pltpu.make_async_remote_copy(
            src_ref=source,
            dst_ref=target,
            send_sem=pair_send.at[phase],
            recv_sem=pair_recv.at[phase],
            device_id={"pb": peer},
            device_id_type=pl.DeviceIdType.MESH,
        )
        copy.start()
        return copy

    def finish(copies):
        for copy in copies:
            copy.wait()

    def load(number, keys):
        source = pl.ds(pl.multiple_of(lax.rem(pb_me + number, pb_size) * block, block), block)
        hbm, vmem, kind = (keys_hbm, keys_v, 0) if keys else (values_hbm, values_v, 1)
        return pltpu.make_async_copy(
            hbm.at[source], vmem.at[number], load_sems.at[kind, number]
        )

    query_load = pltpu.make_async_copy(
        queries_hbm, queries_all.at[pb_me], load_sems.at[2, 0]
    )
    load(0, True).start()
    query_load.start()
    for number in range(pb_size):
        if number > 0:
            load(number, True).start()
        load(number, False).start()

    def pack(target, top, total):
        for piece in range(pieces):
            lanes = slice(piece * 128, (piece + 1) * 128)
            target[piece : piece + 1, :] = top[:, lanes]
            target[pieces + piece : pieces + piece + 1, :] = total[:, lanes]

    def unpack(value):
        return jnp.concatenate([value[piece : piece + 1] for piece in range(pieces)], axis=1)

    load(0, True).wait()
    place = index_ref[pl.ds(pb_me, 1), :] - (ka_me * cache_rows + pb_me * block)
    place = jnp.broadcast_to(place.astype(jnp.float32), (group, group)).T
    first_row = lax.broadcasted_iota(jnp.int32, (group, group), 0) * stride
    offset_row = place - first_row.astype(jnp.float32)
    kept = jnp.zeros((group, width), jnp.float32)
    for step in range(stride):
        kept = jnp.where(
            offset_row == float(step), keys_v[0, pl.ds(step, group, stride=stride), :], kept
        )
    kept_all[ka_me] = kept

    pl.semaphore_wait(barrier, ka_size + pb_size - 2)
    low_peer = ka_me + 1 - 2 * lax.rem(ka_me, 2)

    def kept_copy(offset, source, peer):
        return pltpu.make_async_remote_copy(
            src_ref=kept_all.at[source],
            dst_ref=kept_all.at[source],
            send_sem=ka_send.at[0, offset],
            recv_sem=ka_recv.at[0, offset],
            device_id={"ka": peer},
            device_id_type=pl.DeviceIdType.MESH,
        )

    far = [offset for offset in order_of(ka_size) if offset % 2 == 0]
    far_copies = [kept_copy(offset, ka_me, peer_of("ka", offset)) for offset in far]
    kept_copies = [kept_copy(1, ka_me, low_peer)]
    for copy in far_copies + kept_copies:
        copy.start()
    query_load.wait()
    query_copies = begin("pb", 0, lambda peer: queries_all.at[pb_me], queries_all.at[pb_me])

    own_wide = wide_queries(queries_all[pb_me] * exponent_scale)

    def target_block(number, carry):
        if carry is None:
            scores = product(wide_keys(keys_v[number]), own_wide, 1, 1)
            top_next = jnp.max(scores, axis=0, keepdims=True)
        else:
            load(number, True).wait()
            scores = product(wide_keys(keys_v[number]), own_wide, 1, 1)
            top, total = carry
            top_next = jnp.maximum(top, jnp.max(scores, axis=0, keepdims=True))
            factor = jnp.exp2(top - top_next)
        load(number, False).wait()
        high, low = halves(values_v[number].T)
        exponent = jnp.exp2(scores - top_next)
        block_total = jnp.sum(exponent, axis=0, keepdims=True)
        first, second = halves(exponent)
        both = product(jnp.concatenate((high, low), axis=0), first)
        added = both[:width] + (both[width:] + product(high, second))
        if carry is None:
            sums[...] = added
            return top_next, block_total
        sums[...] = sums[...] * factor + added
        return top_next, total * factor + block_total

    carry = lax.fori_loop(1, 2, target_block, target_block(0, None))
    for offset, copy in zip(far, far_copies):
        copy.wait()
        source = lax.rem(ka_me + ka_size - offset, ka_size)
        forwarded = kept_copy(offset + 1, source, low_peer)
        forwarded.start()
        kept_copies.append(forwarded)
    top, total = lax.fori_loop(2, pb_size, target_block, carry)
    part[...] = sums[...].reshape(ka_size, columns, query_rows)
    pack(stats, top, total)
    stats_copies = begin("ka", 2, lambda peer: stats, stats_in.at[ka_me])
    part_copies = begin("ka", 1, lambda peer: part.at[peer], part_in.at[ka_me])
    part_copies = list(zip(order_of(ka_size), part_copies))
    part_in[ka_me] = part[ka_me]
    stats_in[ka_me] = stats[...]

    finish(query_copies)
    finish(kept_copies)
    kept_wide = wide_keys(kept_all[...].reshape(ka_size * group, width))

    @pl.loop(0, pb_size)
    def _(number):
        queries_wide[...] = wide_queries(queries_all[number] * exponent_scale)
        scores = product(kept_wide, queries_wide[...], 1, 1)
        top = jnp.max(scores, axis=0, keepdims=True)
        exponent = jnp.exp2(scores - top)
        pack(kept_stats.at[pb_me, number], top, jnp.sum(exponent, axis=0, keepdims=True))
        one, two = halves(exponent)
        first_part[number] = one
        second_part[number] = two
        first_turned[number] = one.T
        second_turned[number] = two.T

    kept_stats_copies = begin("pb", 1, lambda peer: kept_stats.at[pb_me], kept_stats.at[pb_me])

    finish(stats_copies)
    joint_top = stats_in[0, :pieces]
    for source in range(1, ka_size):
        joint_top = jnp.maximum(joint_top, stats_in[source, :pieces])
    joint_total = jnp.zeros_like(joint_top)
    for source in range(ka_size):
        joint_total = joint_total + stats_in[source, pieces:] * jnp.exp2(
            stats_in[source, :pieces] - joint_top
        )

    def weighted(source):
        return part_in[source] * unpack(jnp.exp2(stats_in[source, :pieces] - joint_top))

    numerator = weighted(ka_me)
    for offset, copy in part_copies:
        copy.wait()
        numerator = numerator + weighted(lax.rem(ka_me + ka_size - offset, ka_size))
    target_all[pb_me] = numerator / unpack(joint_total)
    target_copies = begin("pb", 2, lambda peer: target_all.at[pb_me], target_all.at[pb_me])

    finish(kept_stats_copies)
    for number in range(pb_size):
        joint_top = kept_stats[0, number, :pieces]
        for source in range(1, pb_size):
            joint_top = jnp.maximum(joint_top, kept_stats[source, number, :pieces])
        joint_total = jnp.zeros_like(joint_top)
        for source in range(pb_size):
            joint_total = joint_total + kept_stats[source, number, pieces:] * jnp.exp2(
                kept_stats[source, number, :pieces] - joint_top
            )
        own_top = kept_stats[pb_me, number, :pieces]
        scale[number] = jnp.broadcast_to(
            unpack(jnp.exp2(own_top - joint_top) / joint_total), (columns, query_rows)
        )

    def backward(number, vector):
        rows = stacked(scale[number] * vector)
        return product(rows, first_turned[number]) + product(rows, second_turned[number])

    lane = lax.broadcasted_iota(jnp.int32, (columns, 128), 1)

    def lane_sums(value):
        return jnp.sum(value, axis=1, keepdims=True)

    def long(number):
        return query_rows + 128 if number == 0 else query_rows

    def forward(phase, slot, vector, tail):
        rows = stacked(vector)

        def chunk_of(half, number):
            chunk = 2 * half + number
            term = folded(product(rows, first_part[chunk]) + product(rows, second_part[chunk]))
            half_out[slot, half, number, :, :query_rows] = scale[chunk] * term
            if number == 0:
                half_out[slot, half, number, :, query_rows:] = tail

        core_copies = []
        for number in range(2):
            chunk_of(1 - core_bit, number)
            lanes = pl.ds(0, long(number))
            core_copies.append(
                pair(
                    phase + number,
                    core_peer,
                    half_out.at[slot, 1 - core_bit, number, :, lanes],
                    core_in.at[slot, number, :, lanes],
                )
            )
        side_copies = []
        for number in range(2):
            chunk_of(core_bit, number)
            core_copies[number].wait()
            lanes = pl.ds(0, long(number))
            side_out[slot, number, :, lanes] = (
                half_out[slot, core_bit, number, :, lanes] + core_in[slot, number, :, lanes]
            )
            side_copies.append(
                pair(
                    phase + 2 + number,
                    side_peer,
                    side_out.at[slot, number, :, lanes],
                    side_in.at[slot, number, :, lanes],
                )
            )
        return side_copies

    def spread(phase, slot, value):
        for target in range(ka_size):
            piece_out[slot, target] = value[:, target * group : (target + 1) * group]
        piece_in[slot, ka_me] = piece_out[slot, ka_me]
        return begin(
            "ka", phase, lambda peer: piece_out.at[slot, peer], piece_in.at[slot, ka_me]
        )

    def share(phase, slot):
        blocks_all[slot, pb_me] = piece_in[slot].reshape(width, group)
        return begin(
            "pb", phase, lambda peer: blocks_all.at[slot, pb_me], blocks_all.at[slot, pb_me]
        )

    factor_place[...] = jnp.zeros_like(factor_place)
    image = backward(pb_me, target_all[pb_me])
    for offset, copy in sorted(
        zip(order_of(pb_size), target_copies), key=lambda item: item[0] % 2, reverse=True
    ):
        copy.wait()
        source = lax.rem(pb_me + pb_size - offset, pb_size)
        image = image + backward(source, target_all[source])
    residual = folded(image)
    residual_v[...] = residual
    side_copies = forward(
        0, 0, residual, jnp.where(lane == 0, lane_sums(residual * residual), 0.0)
    )
    spread_copies = spread(3, 0, residual)
    update_copies = []
    for number in range(2):
        side_copies[number].wait()
        joined = side_out[0, number, :, :query_rows] + side_in[0, number, :, :query_rows]
        updates_all[2 * core_bit + number] = joined
        update_copies.append(
            pair(
                4 + number,
                core_peer,
                updates_all.at[2 * core_bit + number],
                updates_all.at[2 * core_bit + number],
            )
        )
    norm_first = (side_out[0, 0, :, query_rows:] + side_in[0, 0, :, query_rows:])[:, :1]
    image = None
    energy = None
    for half in (core_bit, 1 - core_bit):
        for number in range(2):
            if half is not core_bit:
                update_copies[number].wait()
            updates = updates_all[2 * half + number]
            term = backward(2 * half + number, updates)
            image = term if image is None else image + term
            term = lane_sums(updates * updates)
            energy = term if energy is None else energy + term
        if half is core_bit:
            finish(spread_copies)
            first_copies = share(3, 0)
    step_first = norm_first / (energy + ridge_weight * norm_first)
    residual = residual_v[...]
    after = residual - step_first * (folded(image) + ridge_weight * residual)
    spread_copies = spread(4, 1, after)
    tail = jnp.where(
        lane == 0,
        lane_sums(after * after),
        jnp.where(lane == 1, lane_sums(after * residual), 0.0),
    )
    side_copies = forward(6, 1, after, tail)
    finish(side_copies)
    tail = side_out[1, 0, :, query_rows:] + side_in[1, 0, :, query_rows:]
    norm_second = tail[:, :1]
    ratio = norm_second / norm_first
    energy = None
    for number in range(2):
        updates = side_out[1, number, :, :query_rows] + side_in[1, number, :, :query_rows]
        updates = updates + ratio * updates_all[2 * core_bit + number]
        term = lane_sums(updates * updates)
        energy = term if energy is None else energy + term
    energy_out[...] = jnp.broadcast_to(energy, energy_out.shape)
    energy_copy = pair(10, core_peer, energy_out, energy_in)
    finish(spread_copies)
    second_copies = share(4, 1)
    energy_copy.wait()
    energy = energy_out[:, :1] + energy_in[:, :1]
    length = norm_second + 2.0 * ratio * tail[:, 1:2] + ratio * ratio * norm_first
    step_second = norm_second / (energy + ridge_weight * length)
    factor_place[pl.ds(pl.multiple_of(ka_me * columns, columns), columns), :] = jnp.where(
        lane == 0, step_first + step_second * ratio, step_second
    )
    factors[ka_me] = factor_place[...].T[:2]
    factor_copies = begin("ka", 5, lambda peer: factors.at[ka_me], factors.at[ka_me])
    finish(first_copies)
    finish(second_copies)
    turned = [[blocks_all[slot, number].T for number in range(pb_size)] for slot in range(2)]
    finish(factor_copies)
    both = factors[0]
    for source in range(1, ka_size):
        both = both + factors[source]
    for number in range(pb_size):
        fitted_ref[number * group : (number + 1) * group, :] = (
            both[0:1] * turned[0][number] + both[1:2] * turned[1][number]
        )


def whole(queries, cache_keys, cache_values, kept_index, exponent_scale):
    ka_size, pb_size = lax.axis_size("ka"), lax.axis_size("pb")
    query_rows, width = queries.shape
    kept_rows = kept_index.shape[0]
    cache_rows = cache_keys.shape[0]
    group, block, columns = kept_rows // pb_size, cache_rows // pb_size, width // ka_size
    pieces = query_rows // 128
    joint = ka_size * group
    space = functools.partial(pltpu.VMEM, dtype=jnp.float32)
    narrow = functools.partial(pltpu.VMEM, dtype=jnp.bfloat16)
    return pl.pallas_call(
        functools.partial(whole_kernel, ka_size, pb_size, exponent_scale),
        out_shape=jax.ShapeDtypeStruct((kept_rows, width), jnp.float32),
        in_specs=[pl.BlockSpec(memory_space=pltpu.VMEM)]
        + [pl.BlockSpec(memory_space=pl.ANY)] * 3,
        out_specs=pl.BlockSpec(memory_space=pltpu.VMEM),
        scratch_shapes=[
            space((pb_size, block, width)),
            space((pb_size, block, width)),
            space((width, query_rows)),
            space((pb_size, query_rows, width)),
            narrow((query_rows, 6 * width)),
            space((ka_size, group, width)),
            space((ka_size, columns, query_rows)),
            space((ka_size, columns, query_rows)),
            space((2 * pieces, 128)),
            space((ka_size, 2 * pieces, 128)),
            narrow((pb_size, joint, query_rows)),
            narrow((pb_size, joint, query_rows)),
            narrow((pb_size, query_rows, joint)),
            narrow((pb_size, query_rows, joint)),
            space((pb_size, pb_size, 2 * pieces, 128)),
            space((pb_size, columns, query_rows)),
            space((pb_size, columns, query_rows)),
            space((columns, joint)),
            space((2, 2, 2, columns, query_rows + 128)),
            space((2, 2, columns, query_rows + 128)),
            space((2, 2, columns, query_rows + 128)),
            space((2, 2, columns, query_rows + 128)),
            space((pb_size, columns, query_rows)),
            space((columns, 128)),
            space((columns, 128)),
            space((2, ka_size, columns, group)),
            space((2, ka_size, columns, group)),
            space((2, pb_size, width, group)),
            space((width, 128)),
            space((ka_size, 2, 128)),
            pltpu.SemaphoreType.DMA((3, pb_size)),
            pltpu.SemaphoreType.DMA((6, ka_size)),
            pltpu.SemaphoreType.DMA((6, ka_size)),
            pltpu.SemaphoreType.DMA((5, pb_size)),
            pltpu.SemaphoreType.DMA((5, pb_size)),
            pltpu.SemaphoreType.DMA((11,)),
            pltpu.SemaphoreType.DMA((11,)),
        ],
        compiler_params=pltpu.CompilerParams(
            collective_id=1, has_side_effects=True, vmem_limit_bytes=107 * 512 * 1024
        ),
    )(kept_index.reshape(pb_size, group), queries, cache_keys, cache_values)


def suits(ka_size, pb_size, queries, cache_keys, kept_index):
    width = queries.shape[1]
    group = kept_index.shape[0] // pb_size
    return (
        pb_size == 4
        and width == 128
        and group == 128
        and queries.shape[0] == 512
        and cache_keys.shape[0] == 8192
        and width % (8 * ka_size) == 0
    )


def shards(queries, cache_keys, cache_values, kept_index):
    head_width = queries.shape[1]
    inverse_root = 1.0 / math.sqrt(head_width)
    cache_rows = cache_keys.shape[0]
    if suits(lax.axis_size("ka"), lax.axis_size("pb"), queries, cache_keys, kept_index):
        exponent_scale = inverse_root * math.log2(math.e)
        return whole(queries, cache_keys, cache_values, kept_index, exponent_scale)

    local_kept = kept_index - lax.axis_index("ka") * cache_rows
    kept_keys = jnp.take(cache_keys, local_kept, axis=0)
    kept_scores = contract(queries, kept_keys, 1, 1) * inverse_root
    kept_top = jnp.max(kept_scores, axis=1)
    kept_exponent = jnp.exp(kept_scores - kept_top[:, None])
    kept_total = jnp.sum(kept_exponent, axis=1)

    zero = jnp.zeros_like(kept_top)
    stats = jnp.stack((zero, zero, kept_top, kept_total), axis=1)
    stats = jnp.pad(stats, ((0, 0), (0, head_width - 4)))
    return fit(
        target_part(queries, cache_keys, cache_values, stats, inverse_root), kept_exponent
    )


def solution(mesh):
    in_specs = (P("pb", None), P("ka", None), P("ka", None), P("ka"))
    out_specs = P("ka", None)
    return jax.shard_map(shards, mesh=mesh, in_specs=in_specs, out_specs=out_specs, check_vma=False)
```

```python
import functools
import math

import jax
import jax.numpy as jnp
from jax import lax
from jax.experimental import pallas as pl
from jax.experimental.pallas import tpu as pltpu
from jax.sharding import PartitionSpec as P

ITERS = 2


ridge_weight = 0.01
highest = lax.Precision.HIGHEST


def contract(left_side, right_side, left_dim, right_dim):
    return lax.dot_general(
        left_side,
        right_side,
        (((left_dim,), (right_dim,)), ((), ())),
        precision=highest,
        preferred_element_type=jnp.float32,
    )


def column_sums(left_side, right_side):
    return jnp.sum(left_side * right_side, axis=0, keepdims=True)


def fit_kernel(
    ka_size,
    pb_size,
    part_ref,
    kept_ref,
    fitted_ref,
    flipped,
    stats_in,
    stats_all,
    ka_out,
    ka_in,
    ka_all,
    pb_out,
    pb_in,
    pb_all,
    tail_out,
    tail_in,
    ka_send,
    ka_recv,
    pb_send,
    pb_recv,
):
    ka_me = lax.axis_index("ka")
    pb_me = lax.axis_index("pb")
    width = fitted_ref.shape[1]
    query_rows = kept_ref.shape[0]
    kept_rows = kept_ref.shape[1]
    ka_share = query_rows // ka_size
    pb_share = kept_rows // pb_size

    def peer_of(axis, offset):
        size = ka_size if axis == "ka" else pb_size
        me = ka_me if axis == "ka" else pb_me
        return lax.rem(me + offset, size)

    barrier = pltpu.get_barrier_semaphore()
    for axis, size in (("ka", ka_size), ("pb", pb_size)):
        for offset in range(1, size):
            pl.semaphore_signal(
                barrier,
                inc=1,
                device_id={axis: peer_of(axis, offset)},
                device_id_type=pl.DeviceIdType.MESH,
            )
    pl.semaphore_wait(barrier, ka_size + pb_size - 2)

    def begin(axis, phase, source_of, target):
        size, send, recv = (
            (ka_size, ka_send, ka_recv) if axis == "ka" else (pb_size, pb_send, pb_recv)
        )
        copies = []
        for offset in range(1, size):
            peer = peer_of(axis, offset)
            copy = pltpu.make_async_remote_copy(
                src_ref=source_of(peer),
                dst_ref=target,
                send_sem=send.at[phase, offset],
                recv_sem=recv.at[phase, offset],
                device_id={axis: peer},
                device_id_type=pl.DeviceIdType.MESH,
            )
            copy.start()
            copies.append(copy)
        return copies

    def finish(copies):
        for copy in copies:
            copy.wait()

    def scattered_sum(axis, phase, value, tail, out, arrived, whole):
        me, size, share = (
            (ka_me, ka_size, ka_share) if axis == "ka" else (pb_me, pb_size, pb_share)
        )
        out[:, :share, :] = value.reshape(size, share, width)
        out[:, share:, :] = jnp.broadcast_to(tail[None], (size, 8, width))
        copies = begin(axis, phase, lambda peer: out.at[peer], arrived.at[me])
        arrived[me] = out[me]
        finish(copies)
        total = arrived[0]
        for source in range(1, size):
            total = total + arrived[source]
        whole[me] = total[:share]
        finish(begin(axis, phase + 1, lambda peer: whole.at[me], whole.at[me]))
        return whole[...].reshape(size * share, width), total[share:]

    def matmul(left_side, right_side):
        return jnp.dot(
            left_side, right_side, precision=highest, preferred_element_type=jnp.float32
        )

    def tail_rows(*rows):
        place = lax.broadcasted_iota(jnp.int32, (8, width), 0)
        tail = jnp.zeros((8, width), jnp.float32)
        for number, row in enumerate(rows):
            tail = jnp.where(place == number, row, tail)
        return tail

    copies = begin("ka", 0, lambda peer: part_ref.at[peer], stats_in.at[ka_me])
    stats_in[ka_me] = part_ref[ka_me]
    flipped[...] = kept_ref[...].T
    finish(copies)

    def column(source, number):
        return stats_in[source, :, width + number : width + number + 1]

    top = column(0, 0)
    kept_top = column(0, 2)
    for source in range(1, ka_size):
        top = jnp.maximum(top, column(source, 0))
        kept_top = jnp.maximum(kept_top, column(source, 2))
    total = jnp.zeros_like(top)
    kept_total = jnp.zeros_like(top)
    numerator = jnp.zeros((ka_share, width), jnp.float32)
    for source in range(ka_size):
        factor = jnp.exp(column(source, 0) - top)
        total = total + column(source, 1) * factor
        numerator = numerator + stats_in[source, :, :width] * factor
        kept_total = kept_total + column(source, 3) * jnp.exp(column(source, 2) - kept_top)
    lane = lax.broadcasted_iota(jnp.int32, (ka_share, width), 1)
    stats_all[ka_me, :, :width] = numerator / total
    stats_all[ka_me, :, width:] = jnp.where(lane == 0, kept_top, kept_total)
    finish(begin("ka", 1, lambda peer: stats_all.at[ka_me], stats_all.at[ka_me]))
    target = stats_all[:, :, :width].reshape(query_rows, width)
    joint_top = stats_all[:, :, width : width + 1].reshape(query_rows, 1)
    joint_total = stats_all[:, :, width + 1 : width + 2].reshape(query_rows, 1)
    own_top = part_ref[:, :, width + 2 : width + 3].reshape(query_rows, 1)
    scale = jnp.exp(own_top - joint_top) / joint_total

    no_tail = jnp.zeros((8, width), jnp.float32)
    residual, _ = scattered_sum(
        "pb",
        0,
        matmul(flipped[...], scale * target),
        no_tail,
        pb_out.at[0],
        pb_in.at[0],
        pb_all.at[0],
    )
    fitted = jnp.zeros_like(residual)
    direction = residual
    updates = None
    norm_now = None
    length_now = None
    for iteration in range(ITERS):
        forward = scale * matmul(kept_ref[...], residual)
        tail = tail_rows(column_sums(residual, residual), column_sums(residual, direction))
        summed, tail = scattered_sum(
            "ka",
            2 + 2 * iteration,
            forward,
            tail,
            ka_out.at[iteration],
            ka_in.at[iteration],
            ka_all.at[iteration],
        )
        norm_next = tail[0:1]
        if iteration == 0:
            updates = summed
            length_now = norm_next
        else:
            ratio = norm_next / norm_now
            direction = residual + ratio * direction
            updates = summed + ratio * updates
            length_now = norm_next + 2.0 * ratio * tail[1:2] + ratio * ratio * length_now
        norm_now = norm_next
        energy = tail_rows(column_sums(updates, updates))
        if iteration + 1 == ITERS:
            tail_out[...] = energy
            copies = begin("pb", 2 * ITERS, lambda peer: tail_out, tail_in.at[pb_me])
            tail_in[pb_me] = energy
            finish(copies)
            energy = tail_in[0]
            for source in range(1, pb_size):
                energy = energy + tail_in[source]
            step_length = norm_now / (energy[0:1] + ridge_weight * length_now)
            fitted_ref[...] = fitted + step_length * direction
        else:
            image, energy = scattered_sum(
                "pb",
                2 + 2 * iteration,
                matmul(flipped[...], scale * updates),
                energy,
                pb_out.at[iteration + 1],
                pb_in.at[iteration + 1],
                pb_all.at[iteration + 1],
            )
            step_length = norm_now / (energy[0:1] + ridge_weight * length_now)
            fitted = fitted + step_length * direction
            residual = residual - step_length * (image + ridge_weight * direction)


def fit(part, kept_exponent):
    ka_size, pb_size = lax.axis_size("ka"), lax.axis_size("pb")
    query_rows, kept_rows = kept_exponent.shape
    width = part.shape[1] // 2
    ka_share, pb_share = query_rows // ka_size, kept_rows // pb_size
    space = functools.partial(pltpu.VMEM, dtype=jnp.float32)
    return pl.pallas_call(
        functools.partial(fit_kernel, ka_size, pb_size),
        out_shape=jax.ShapeDtypeStruct((kept_rows, width), jnp.float32),
        in_specs=[pl.BlockSpec(memory_space=pltpu.VMEM)] * 2,
        out_specs=pl.BlockSpec(memory_space=pltpu.VMEM),
        scratch_shapes=[
            space((kept_rows, query_rows)),
            space((ka_size, ka_share, 2 * width)),
            space((ka_size, ka_share, 2 * width)),
            space((ITERS, ka_size, ka_share + 8, width)),
            space((ITERS, ka_size, ka_share + 8, width)),
            space((ITERS, ka_size, ka_share, width)),
            space((ITERS, pb_size, pb_share + 8, width)),
            space((ITERS, pb_size, pb_share + 8, width)),
            space((ITERS, pb_size, pb_share, width)),
            space((8, width)),
            space((pb_size, 8, width)),
            pltpu.SemaphoreType.DMA((2 + 2 * ITERS, ka_size)),
            pltpu.SemaphoreType.DMA((2 + 2 * ITERS, ka_size)),
            pltpu.SemaphoreType.DMA((2 * ITERS + 1, pb_size)),
            pltpu.SemaphoreType.DMA((2 * ITERS + 1, pb_size)),
        ],
        compiler_params=pltpu.CompilerParams(
            collective_id=0, has_side_effects=True, vmem_limit_bytes=40 * 1024 * 1024
        ),
    )(part.reshape(ka_size, ka_share, 2 * width), kept_exponent)


def thirds(value):
    first = value.astype(jnp.bfloat16)
    rest = value - first.astype(jnp.float32)
    second = rest.astype(jnp.bfloat16)
    third = (rest - second.astype(jnp.float32)).astype(jnp.bfloat16)
    return first, second, third


def target_kernel(inverse_root, queries_ref, keys_ref, values_ref, kept_ref, part_ref, wide, top, total, sums):
    width = queries_ref.shape[1]

    @pl.when(pl.program_id(0) == 0)
    def _():
        one, two, three = thirds(queries_ref[...])
        wide[...] = jnp.concatenate((one, one, two, one, three, two), axis=1)
        top[...] = jnp.full_like(top, -jnp.inf)
        total[...] = jnp.zeros_like(total)
        sums[...] = jnp.zeros_like(sums)

    one, two, three = thirds(keys_ref[...])
    scores = (
        lax.dot_general(
            wide[...],
            jnp.concatenate((one, two, one, three, one, two), axis=1),
            (((1,), (1,)), ((), ())),
            preferred_element_type=jnp.float32,
        )
        * inverse_root
    )
    top_next = jnp.maximum(top[...], jnp.max(scores, axis=1, keepdims=True))
    factor = jnp.exp(top[...] - top_next)
    exponent = jnp.exp(scores - top_next)
    top[...] = top_next
    total[...] = total[...] * factor + jnp.sum(exponent, axis=1, keepdims=True)
    one, two, three = thirds(values_ref[...])
    high, middle, low = thirds(exponent)
    pair = jnp.concatenate((one, two), axis=1)
    product = functools.partial(jnp.dot, preferred_element_type=jnp.float32)
    both = product(high, pair) + product(middle, pair)
    small = product(high, three) + product(low, one)
    sums[...] = sums[...] * factor + (both[:, :width] + (both[:, width:] + small))

    @pl.when(pl.program_id(0) == pl.num_programs(0) - 1)
    def _():
        lane = lax.broadcasted_iota(jnp.int32, kept_ref.shape, 1)
        stats = jnp.where(lane == 0, top[...], jnp.where(lane == 1, total[...], kept_ref[...]))
        part_ref[:, :width] = sums[...]
        part_ref[:, width:] = stats


def target_part(queries, cache_keys, cache_values, kept_stats, inverse_root):
    query_rows, width = queries.shape
    block_size = min(2048, cache_keys.shape[0])
    fixed = pl.BlockSpec((query_rows, width), lambda block: (0, 0))
    moving = pl.BlockSpec((block_size, width), lambda block: (block, 0))
    return pl.pallas_call(
        functools.partial(target_kernel, inverse_root),
        grid=(cache_keys.shape[0] // block_size,),
        out_shape=jax.ShapeDtypeStruct((query_rows, 2 * width), jnp.float32),
        in_specs=[fixed, moving, moving, fixed],
        out_specs=pl.BlockSpec((query_rows, 2 * width), lambda block: (0, 0)),
        scratch_shapes=[
            pltpu.VMEM((query_rows, 6 * width), jnp.bfloat16),
            pltpu.VMEM((query_rows, 1), jnp.float32),
            pltpu.VMEM((query_rows, 1), jnp.float32),
            pltpu.VMEM((query_rows, width), jnp.float32),
        ],
        compiler_params=pltpu.CompilerParams(vmem_limit_bytes=40 * 1024 * 1024),
    )(queries, cache_keys, cache_values, kept_stats)


def halves(value):
    first = value.astype(jnp.bfloat16)
    return first, (value - first.astype(jnp.float32)).astype(jnp.bfloat16)


def product(left_side, right_side, left_dim=1, right_dim=0):
    return lax.dot_general(
        left_side,
        right_side,
        (((left_dim,), (right_dim,)), ((), ())),
        preferred_element_type=jnp.float32,
    )


def wide_queries(value):
    one, two, three = thirds(value)
    return jnp.concatenate((one, one, two, one, three, two), axis=1)


def wide_keys(value):
    one, two, three = thirds(value)
    return jnp.concatenate((one, two, one, three, one, two), axis=1)


def stacked(value):
    return jnp.concatenate(thirds(value), axis=0)


def folded(value):
    rows = value.shape[0] // 3
    return value[:rows] + (value[rows : 2 * rows] + value[2 * rows :])


def order_of(size):
    return list(range(1, size))


def whole_kernel(
    ka_size,
    pb_size,
    exponent_scale,
    index_ref,
    queries_hbm,
    keys_hbm,
    values_hbm,
    fitted_ref,
    keys_v,
    values_v,
    sums,
    queries_all,
    queries_wide,
    kept_all,
    part,
    part_in,
    stats,
    stats_in,
    first_part,
    second_part,
    first_turned,
    second_turned,
    kept_stats,
    scale,
    target_all,
    residual_v,
    half_out,
    core_in,
    side_out,
    side_in,
    updates_all,
    energy_out,
    energy_in,
    piece_out,
    piece_in,
    blocks_all,
    factor_place,
    factors,
    load_sems,
    ka_send,
    ka_recv,
    pb_send,
    pb_recv,
    pair_send,
    pair_recv,
):
    ka_me = lax.axis_index("ka")
    pb_me = lax.axis_index("pb")
    query_rows, width = queries_hbm.shape
    columns = width // ka_size
    pieces = query_rows // 128
    group = kept_all.shape[1]
    cache_rows = keys_hbm.shape[0]
    block = cache_rows // pb_size
    stride = block // group
    core_bit = lax.rem(pb_me, 2)
    core_peer = pb_me + 1 - 2 * core_bit
    side_peer = lax.rem(pb_me + 2, 4)

    def peer_of(axis, offset):
        if axis == "ka":
            return lax.rem(ka_me + offset, ka_size)
        return lax.rem(pb_me + offset, pb_size)

    barrier = pltpu.get_barrier_semaphore()
    for axis, size in (("ka", ka_size), ("pb", pb_size)):
        for offset in range(1, size):
            pl.semaphore_signal(
                barrier,
                inc=1,
                device_id={axis: peer_of(axis, offset)},
                device_id_type=pl.DeviceIdType.MESH,
            )

    def begin(axis, phase, source_of, target):
        size, send, recv = (
            (ka_size, ka_send, ka_recv) if axis == "ka" else (pb_size, pb_send, pb_recv)
        )
        copies = []
        for offset in order_of(size):
            peer = peer_of(axis, offset)
            copy = pltpu.make_async_remote_copy(
                src_ref=source_of(peer),
                dst_ref=target,
                send_sem=send.at[phase, offset],
                recv_sem=recv.at[phase, offset],
                device_id={axis: peer},
                device_id_type=pl.DeviceIdType.MESH,
            )
            copy.start()
            copies.append(copy)
        return copies

    def pair(phase, peer, source, target):
        copy = pltpu.make_async_remote_copy(
            src_ref=source,
            dst_ref=target,
            send_sem=pair_send.at[phase],
            recv_sem=pair_recv.at[phase],
            device_id={"pb": peer},
            device_id_type=pl.DeviceIdType.MESH,
        )
        copy.start()
        return copy

    def finish(copies):
        for copy in copies:
            copy.wait()

    def load(number, keys):
        source = pl.ds(pl.multiple_of(lax.rem(pb_me + number, pb_size) * block, block), block)
        hbm, vmem, kind = (keys_hbm, keys_v, 0) if keys else (values_hbm, values_v, 1)
        return pltpu.make_async_copy(
            hbm.at[source], vmem.at[number], load_sems.at[kind, number]
        )

    query_load = pltpu.make_async_copy(
        queries_hbm, queries_all.at[pb_me], load_sems.at[2, 0]
    )
    load(0, True).start()
    query_load.start()

    def pack(target, top, total):
        for piece in range(pieces):
            lanes = slice(piece * 128, (piece + 1) * 128)
            target[piece : piece + 1, :] = top[:, lanes]
            target[pieces + piece : pieces + piece + 1, :] = total[:, lanes]

    def unpack(value):
        return jnp.concatenate([value[piece : piece + 1] for piece in range(pieces)], axis=1)

    load(0, True).wait()
    for number in range(pb_size):
        if number > 0:
            load(number, True).start()
        load(number, False).start()
    place = index_ref[pl.ds(pb_me, 1), :] - (ka_me * cache_rows + pb_me * block)
    place = jnp.broadcast_to(place.astype(jnp.float32), (group, group)).T
    first_row = lax.broadcasted_iota(jnp.int32, (group, group), 0) * stride
    offset_row = place - first_row.astype(jnp.float32)
    kept = jnp.zeros((group, width), jnp.float32)
    for step in range(stride):
        kept = jnp.where(
            offset_row == float(step), keys_v[0, pl.ds(step, group, stride=stride), :], kept
        )
    kept_all[ka_me] = kept

    pl.semaphore_wait(barrier, ka_size + pb_size - 2)
    low_peer = ka_me + 1 - 2 * lax.rem(ka_me, 2)

    def kept_copy(offset, source, peer):
        return pltpu.make_async_remote_copy(
            src_ref=kept_all.at[source],
            dst_ref=kept_all.at[source],
            send_sem=ka_send.at[0, offset],
            recv_sem=ka_recv.at[0, offset],
            device_id={"ka": peer},
            device_id_type=pl.DeviceIdType.MESH,
        )

    far = [offset for offset in order_of(ka_size) if offset % 2 == 0]
    far_copies = [kept_copy(offset, ka_me, peer_of("ka", offset)) for offset in far]
    kept_copies = [kept_copy(1, ka_me, low_peer)]
    for copy in far_copies + kept_copies:
        copy.start()
    query_load.wait()
    query_copies = begin("pb", 0, lambda peer: queries_all.at[pb_me], queries_all.at[pb_me])

    own_wide = wide_queries(queries_all[pb_me] * exponent_scale)

    def target_block(number, carry):
        if carry is None:
            scores = product(wide_keys(keys_v[number]), own_wide, 1, 1)
            top_next = jnp.max(scores, axis=0, keepdims=True)
        else:
            load(number, True).wait()
            scores = product(wide_keys(keys_v[number]), own_wide, 1, 1)
            top, total = carry
            top_next = jnp.maximum(top, jnp.max(scores, axis=0, keepdims=True))
            factor = jnp.exp2(top - top_next)
        load(number, False).wait()
        high, low = halves(values_v[number].T)
        exponent = jnp.exp2(scores - top_next)
        block_total = jnp.sum(exponent, axis=0, keepdims=True)
        first, second = halves(exponent)
        both = product(jnp.concatenate((high, low), axis=0), first)
        added = both[:width] + (both[width:] + product(high, second))
        if carry is None:
            sums[...] = added
            return top_next, block_total
        sums[...] = sums[...] * factor + added
        return top_next, total * factor + block_total

    carry = lax.fori_loop(1, 2, target_block, target_block(0, None))
    for offset, copy in zip(far, far_copies):
        copy.wait()
        source = lax.rem(ka_me + ka_size - offset, ka_size)
        forwarded = kept_copy(offset + 1, source, low_peer)
        forwarded.start()
        kept_copies.append(forwarded)
    top, total = lax.fori_loop(2, pb_size, target_block, carry)
    part[...] = sums[...].reshape(ka_size, columns, query_rows)
    pack(stats, top, total)
    stats_copies = begin("ka", 2, lambda peer: stats, stats_in.at[ka_me])
    part_copies = begin("ka", 1, lambda peer: part.at[peer], part_in.at[ka_me])
    part_copies = list(zip(order_of(ka_size), part_copies))
    part_in[ka_me] = part[ka_me]
    stats_in[ka_me] = stats[...]

    finish(query_copies)
    finish(kept_copies)
    kept_wide = wide_keys(kept_all[...].reshape(ka_size * group, width))

    @pl.loop(0, pb_size)
    def _(number):
        queries_wide[...] = wide_queries(queries_all[number] * exponent_scale)
        scores = product(kept_wide, queries_wide[...], 1, 1)
        top = jnp.max(scores, axis=0, keepdims=True)
        exponent = jnp.exp2(scores - top)
        pack(kept_stats.at[pb_me, number], top, jnp.sum(exponent, axis=0, keepdims=True))
        one, two = halves(exponent)
        first_part[number] = one
        second_part[number] = two
        first_turned[number] = one.T
        second_turned[number] = two.T

    kept_stats_copies = begin("pb", 1, lambda peer: kept_stats.at[pb_me], kept_stats.at[pb_me])

    finish(stats_copies)
    joint_top = stats_in[0, :pieces]
    for source in range(1, ka_size):
        joint_top = jnp.maximum(joint_top, stats_in[source, :pieces])
    joint_total = jnp.zeros_like(joint_top)
    for source in range(ka_size):
        joint_total = joint_total + stats_in[source, pieces:] * jnp.exp2(
            stats_in[source, :pieces] - joint_top
        )

    def weighted(source):
        return part_in[source] * unpack(jnp.exp2(stats_in[source, :pieces] - joint_top))

    numerator = weighted(ka_me)
    for offset, copy in part_copies:
        copy.wait()
        numerator = numerator + weighted(lax.rem(ka_me + ka_size - offset, ka_size))
    target_all[pb_me] = numerator / unpack(joint_total)
    target_copies = begin("pb", 2, lambda peer: target_all.at[pb_me], target_all.at[pb_me])

    finish(kept_stats_copies)
    for number in range(pb_size):
        joint_top = kept_stats[0, number, :pieces]
        for source in range(1, pb_size):
            joint_top = jnp.maximum(joint_top, kept_stats[source, number, :pieces])
        joint_total = jnp.zeros_like(joint_top)
        for source in range(pb_size):
            joint_total = joint_total + kept_stats[source, number, pieces:] * jnp.exp2(
                kept_stats[source, number, :pieces] - joint_top
            )
        own_top = kept_stats[pb_me, number, :pieces]
        scale[number] = jnp.broadcast_to(
            unpack(jnp.exp2(own_top - joint_top) / joint_total), (columns, query_rows)
        )

    def backward(number, vector):
        rows = stacked(scale[number] * vector)
        return product(rows, first_turned[number]) + product(rows, second_turned[number])

    lane = lax.broadcasted_iota(jnp.int32, (columns, 128), 1)

    def lane_sums(value):
        return jnp.sum(value, axis=1, keepdims=True)

    def long(number):
        return query_rows + 128 if number == 0 else query_rows

    def forward(phase, slot, vector, tail):
        rows = stacked(vector)

        def chunk_of(half, number):
            chunk = 2 * half + number
            term = folded(product(rows, first_part[chunk]) + product(rows, second_part[chunk]))
            half_out[slot, half, number, :, :query_rows] = scale[chunk] * term
            if number == 0:
                half_out[slot, half, number, :, query_rows:] = tail

        core_copies = []
        for number in range(2):
            chunk_of(1 - core_bit, number)
            lanes = pl.ds(0, long(number))
            core_copies.append(
                pair(
                    phase + number,
                    core_peer,
                    half_out.at[slot, 1 - core_bit, number, :, lanes],
                    core_in.at[slot, number, :, lanes],
                )
            )
        side_copies = []
        for number in range(2):
            chunk_of(core_bit, number)
            core_copies[number].wait()
            lanes = pl.ds(0, long(number))
            side_out[slot, number, :, lanes] = (
                half_out[slot, core_bit, number, :, lanes] + core_in[slot, number, :, lanes]
            )
            side_copies.append(
                pair(
                    phase + 2 + number,
                    side_peer,
                    side_out.at[slot, number, :, lanes],
                    side_in.at[slot, number, :, lanes],
                )
            )
        return side_copies

    def spread(phase, slot, value):
        for target in range(ka_size):
            piece_out[slot, target] = value[:, target * group : (target + 1) * group]
        piece_in[slot, ka_me] = piece_out[slot, ka_me]
        return begin(
            "ka", phase, lambda peer: piece_out.at[slot, peer], piece_in.at[slot, ka_me]
        )

    def share(phase, slot):
        blocks_all[slot, pb_me] = piece_in[slot].reshape(width, group)
        return begin(
            "pb", phase, lambda peer: blocks_all.at[slot, pb_me], blocks_all.at[slot, pb_me]
        )

    factor_place[...] = jnp.zeros_like(factor_place)
    image = backward(pb_me, target_all[pb_me])
    for offset, copy in sorted(
        zip(order_of(pb_size), target_copies), key=lambda item: item[0] % 2, reverse=True
    ):
        copy.wait()
        source = lax.rem(pb_me + pb_size - offset, pb_size)
        image = image + backward(source, target_all[source])
    residual = folded(image)
    residual_v[...] = residual
    side_copies = forward(
        0, 0, residual, jnp.where(lane == 0, lane_sums(residual * residual), 0.0)
    )
    spread_copies = spread(3, 0, residual)
    update_copies = []
    for number in range(2):
        side_copies[number].wait()
        joined = side_out[0, number, :, :query_rows] + side_in[0, number, :, :query_rows]
        updates_all[2 * core_bit + number] = joined
        update_copies.append(
            pair(
                4 + number,
                core_peer,
                updates_all.at[2 * core_bit + number],
                updates_all.at[2 * core_bit + number],
            )
        )
    norm_first = (side_out[0, 0, :, query_rows:] + side_in[0, 0, :, query_rows:])[:, :1]
    image = None
    energy = None
    for half in (core_bit, 1 - core_bit):
        for number in range(2):
            if half is not core_bit:
                update_copies[number].wait()
            updates = updates_all[2 * half + number]
            term = backward(2 * half + number, updates)
            image = term if image is None else image + term
            term = lane_sums(updates * updates)
            energy = term if energy is None else energy + term
        if half is core_bit:
            finish(spread_copies)
            first_copies = share(3, 0)
    step_first = norm_first / (energy + ridge_weight * norm_first)
    residual = residual_v[...]
    after = residual - step_first * (folded(image) + ridge_weight * residual)
    spread_copies = spread(4, 1, after)
    tail = jnp.where(
        lane == 0,
        lane_sums(after * after),
        jnp.where(lane == 1, lane_sums(after * residual), 0.0),
    )
    side_copies = forward(6, 1, after, tail)
    finish(side_copies)
    tail = side_out[1, 0, :, query_rows:] + side_in[1, 0, :, query_rows:]
    norm_second = tail[:, :1]
    ratio = norm_second / norm_first
    energy = None
    for number in range(2):
        updates = side_out[1, number, :, :query_rows] + side_in[1, number, :, :query_rows]
        updates = updates + ratio * updates_all[2 * core_bit + number]
        term = lane_sums(updates * updates)
        energy = term if energy is None else energy + term
    energy_out[...] = jnp.broadcast_to(energy, energy_out.shape)
    energy_copy = pair(10, core_peer, energy_out, energy_in)
    finish(spread_copies)
    second_copies = share(4, 1)
    energy_copy.wait()
    energy = energy_out[:, :1] + energy_in[:, :1]
    length = norm_second + 2.0 * ratio * tail[:, 1:2] + ratio * ratio * norm_first
    step_second = norm_second / (energy + ridge_weight * length)
    factor_place[pl.ds(pl.multiple_of(ka_me * columns, columns), columns), :] = jnp.where(
        lane == 0, step_first + step_second * ratio, step_second
    )
    factors[ka_me] = factor_place[...].T[:2]
    factor_copies = begin("ka", 5, lambda peer: factors.at[ka_me], factors.at[ka_me])
    finish(first_copies)
    finish(second_copies)
    turned = [[blocks_all[slot, number].T for number in range(pb_size)] for slot in range(2)]
    finish(factor_copies)
    both = factors[0]
    for source in range(1, ka_size):
        both = both + factors[source]
    for number in range(pb_size):
        fitted_ref[number * group : (number + 1) * group, :] = (
            both[0:1] * turned[0][number] + both[1:2] * turned[1][number]
        )


def whole(queries, cache_keys, cache_values, kept_index, exponent_scale):
    ka_size, pb_size = lax.axis_size("ka"), lax.axis_size("pb")
    query_rows, width = queries.shape
    kept_rows = kept_index.shape[0]
    cache_rows = cache_keys.shape[0]
    group, block, columns = kept_rows // pb_size, cache_rows // pb_size, width // ka_size
    pieces = query_rows // 128
    joint = ka_size * group
    space = functools.partial(pltpu.VMEM, dtype=jnp.float32)
    narrow = functools.partial(pltpu.VMEM, dtype=jnp.bfloat16)
    return pl.pallas_call(
        functools.partial(whole_kernel, ka_size, pb_size, exponent_scale),
        out_shape=jax.ShapeDtypeStruct((kept_rows, width), jnp.float32),
        in_specs=[pl.BlockSpec(memory_space=pltpu.VMEM)]
        + [pl.BlockSpec(memory_space=pl.ANY)] * 3,
        out_specs=pl.BlockSpec(memory_space=pltpu.VMEM),
        scratch_shapes=[
            space((pb_size, block, width)),
            space((pb_size, block, width)),
            space((width, query_rows)),
            space((pb_size, query_rows, width)),
            narrow((query_rows, 6 * width)),
            space((ka_size, group, width)),
            space((ka_size, columns, query_rows)),
            space((ka_size, columns, query_rows)),
            space((2 * pieces, 128)),
            space((ka_size, 2 * pieces, 128)),
            narrow((pb_size, joint, query_rows)),
            narrow((pb_size, joint, query_rows)),
            narrow((pb_size, query_rows, joint)),
            narrow((pb_size, query_rows, joint)),
            space((pb_size, pb_size, 2 * pieces, 128)),
            space((pb_size, columns, query_rows)),
            space((pb_size, columns, query_rows)),
            space((columns, joint)),
            space((2, 2, 2, columns, query_rows + 128)),
            space((2, 2, columns, query_rows + 128)),
            space((2, 2, columns, query_rows + 128)),
            space((2, 2, columns, query_rows + 128)),
            space((pb_size, columns, query_rows)),
            space((columns, 128)),
            space((columns, 128)),
            space((2, ka_size, columns, group)),
            space((2, ka_size, columns, group)),
            space((2, pb_size, width, group)),
            space((width, 128)),
            space((ka_size, 2, 128)),
            pltpu.SemaphoreType.DMA((3, pb_size)),
            pltpu.SemaphoreType.DMA((6, ka_size)),
            pltpu.SemaphoreType.DMA((6, ka_size)),
            pltpu.SemaphoreType.DMA((5, pb_size)),
            pltpu.SemaphoreType.DMA((5, pb_size)),
            pltpu.SemaphoreType.DMA((11,)),
            pltpu.SemaphoreType.DMA((11,)),
        ],
        compiler_params=pltpu.CompilerParams(
            collective_id=1, has_side_effects=True, vmem_limit_bytes=107 * 512 * 1024
        ),
    )(kept_index.reshape(pb_size, group), queries, cache_keys, cache_values)


def suits(ka_size, pb_size, queries, cache_keys, kept_index):
    width = queries.shape[1]
    group = kept_index.shape[0] // pb_size
    return (
        pb_size == 4
        and width == 128
        and group == 128
        and queries.shape[0] == 512
        and cache_keys.shape[0] == 8192
        and width % (8 * ka_size) == 0
    )


def shards(queries, cache_keys, cache_values, kept_index):
    head_width = queries.shape[1]
    inverse_root = 1.0 / math.sqrt(head_width)
    cache_rows = cache_keys.shape[0]
    if suits(lax.axis_size("ka"), lax.axis_size("pb"), queries, cache_keys, kept_index):
        exponent_scale = inverse_root * math.log2(math.e)
        return whole(queries, cache_keys, cache_values, kept_index, exponent_scale)

    local_kept = kept_index - lax.axis_index("ka") * cache_rows
    kept_keys = jnp.take(cache_keys, local_kept, axis=0)
    kept_scores = contract(queries, kept_keys, 1, 1) * inverse_root
    kept_top = jnp.max(kept_scores, axis=1)
    kept_exponent = jnp.exp(kept_scores - kept_top[:, None])
    kept_total = jnp.sum(kept_exponent, axis=1)

    zero = jnp.zeros_like(kept_top)
    stats = jnp.stack((zero, zero, kept_top, kept_total), axis=1)
    stats = jnp.pad(stats, ((0, 0), (0, head_width - 4)))
    return fit(
        target_part(queries, cache_keys, cache_values, stats, inverse_root), kept_exponent
    )


def solution(mesh):
    in_specs = (P("pb", None), P("ka", None), P("ka", None), P("ka"))
    out_specs = P("ka", None)
    return jax.shard_map(shards, mesh=mesh, in_specs=in_specs, out_specs=out_specs, check_vma=False)
```

```python
import functools
import math

import jax
import jax.numpy as jnp
from jax import lax
from jax.experimental import pallas as pl
from jax.experimental.pallas import tpu as pltpu
from jax.sharding import PartitionSpec as P

ITERS = 2


ridge_weight = 0.01
highest = lax.Precision.HIGHEST


def contract(left_side, right_side, left_dim, right_dim):
    return lax.dot_general(
        left_side,
        right_side,
        (((left_dim,), (right_dim,)), ((), ())),
        precision=highest,
        preferred_element_type=jnp.float32,
    )


def column_sums(left_side, right_side):
    return jnp.sum(left_side * right_side, axis=0, keepdims=True)


def fit_kernel(
    ka_size,
    pb_size,
    part_ref,
    kept_ref,
    fitted_ref,
    flipped,
    stats_in,
    stats_all,
    ka_out,
    ka_in,
    ka_all,
    pb_out,
    pb_in,
    pb_all,
    tail_out,
    tail_in,
    ka_send,
    ka_recv,
    pb_send,
    pb_recv,
):
    ka_me = lax.axis_index("ka")
    pb_me = lax.axis_index("pb")
    width = fitted_ref.shape[1]
    query_rows = kept_ref.shape[0]
    kept_rows = kept_ref.shape[1]
    ka_share = query_rows // ka_size
    pb_share = kept_rows // pb_size

    def peer_of(axis, offset):
        size = ka_size if axis == "ka" else pb_size
        me = ka_me if axis == "ka" else pb_me
        return lax.rem(me + offset, size)

    barrier = pltpu.get_barrier_semaphore()
    for axis, size in (("ka", ka_size), ("pb", pb_size)):
        for offset in range(1, size):
            pl.semaphore_signal(
                barrier,
                inc=1,
                device_id={axis: peer_of(axis, offset)},
                device_id_type=pl.DeviceIdType.MESH,
            )
    pl.semaphore_wait(barrier, ka_size + pb_size - 2)

    def begin(axis, phase, source_of, target):
        size, send, recv = (
            (ka_size, ka_send, ka_recv) if axis == "ka" else (pb_size, pb_send, pb_recv)
        )
        copies = []
        for offset in range(1, size):
            peer = peer_of(axis, offset)
            copy = pltpu.make_async_remote_copy(
                src_ref=source_of(peer),
                dst_ref=target,
                send_sem=send.at[phase, offset],
                recv_sem=recv.at[phase, offset],
                device_id={axis: peer},
                device_id_type=pl.DeviceIdType.MESH,
            )
            copy.start()
            copies.append(copy)
        return copies

    def finish(copies):
        for copy in copies:
            copy.wait()

    def scattered_sum(axis, phase, value, tail, out, arrived, whole):
        me, size, share = (
            (ka_me, ka_size, ka_share) if axis == "ka" else (pb_me, pb_size, pb_share)
        )
        out[:, :share, :] = value.reshape(size, share, width)
        out[:, share:, :] = jnp.broadcast_to(tail[None], (size, 8, width))
        copies = begin(axis, phase, lambda peer: out.at[peer], arrived.at[me])
        arrived[me] = out[me]
        finish(copies)
        total = arrived[0]
        for source in range(1, size):
            total = total + arrived[source]
        whole[me] = total[:share]
        finish(begin(axis, phase + 1, lambda peer: whole.at[me], whole.at[me]))
        return whole[...].reshape(size * share, width), total[share:]

    def matmul(left_side, right_side):
        return jnp.dot(
            left_side, right_side, precision=highest, preferred_element_type=jnp.float32
        )

    def tail_rows(*rows):
        place = lax.broadcasted_iota(jnp.int32, (8, width), 0)
        tail = jnp.zeros((8, width), jnp.float32)
        for number, row in enumerate(rows):
            tail = jnp.where(place == number, row, tail)
        return tail

    copies = begin("ka", 0, lambda peer: part_ref.at[peer], stats_in.at[ka_me])
    stats_in[ka_me] = part_ref[ka_me]
    flipped[...] = kept_ref[...].T
    finish(copies)

    def column(source, number):
        return stats_in[source, :, width + number : width + number + 1]

    top = column(0, 0)
    kept_top = column(0, 2)
    for source in range(1, ka_size):
        top = jnp.maximum(top, column(source, 0))
        kept_top = jnp.maximum(kept_top, column(source, 2))
    total = jnp.zeros_like(top)
    kept_total = jnp.zeros_like(top)
    numerator = jnp.zeros((ka_share, width), jnp.float32)
    for source in range(ka_size):
        factor = jnp.exp(column(source, 0) - top)
        total = total + column(source, 1) * factor
        numerator = numerator + stats_in[source, :, :width] * factor
        kept_total = kept_total + column(source, 3) * jnp.exp(column(source, 2) - kept_top)
    lane = lax.broadcasted_iota(jnp.int32, (ka_share, width), 1)
    stats_all[ka_me, :, :width] = numerator / total
    stats_all[ka_me, :, width:] = jnp.where(lane == 0, kept_top, kept_total)
    finish(begin("ka", 1, lambda peer: stats_all.at[ka_me], stats_all.at[ka_me]))
    target = stats_all[:, :, :width].reshape(query_rows, width)
    joint_top = stats_all[:, :, width : width + 1].reshape(query_rows, 1)
    joint_total = stats_all[:, :, width + 1 : width + 2].reshape(query_rows, 1)
    own_top = part_ref[:, :, width + 2 : width + 3].reshape(query_rows, 1)
    scale = jnp.exp(own_top - joint_top) / joint_total

    no_tail = jnp.zeros((8, width), jnp.float32)
    residual, _ = scattered_sum(
        "pb",
        0,
        matmul(flipped[...], scale * target),
        no_tail,
        pb_out.at[0],
        pb_in.at[0],
        pb_all.at[0],
    )
    fitted = jnp.zeros_like(residual)
    direction = residual
    updates = None
    norm_now = None
    length_now = None
    for iteration in range(ITERS):
        forward = scale * matmul(kept_ref[...], residual)
        tail = tail_rows(column_sums(residual, residual), column_sums(residual, direction))
        summed, tail = scattered_sum(
            "ka",
            2 + 2 * iteration,
            forward,
            tail,
            ka_out.at[iteration],
            ka_in.at[iteration],
            ka_all.at[iteration],
        )
        norm_next = tail[0:1]
        if iteration == 0:
            updates = summed
            length_now = norm_next
        else:
            ratio = norm_next / norm_now
            direction = residual + ratio * direction
            updates = summed + ratio * updates
            length_now = norm_next + 2.0 * ratio * tail[1:2] + ratio * ratio * length_now
        norm_now = norm_next
        energy = tail_rows(column_sums(updates, updates))
        if iteration + 1 == ITERS:
            tail_out[...] = energy
            copies = begin("pb", 2 * ITERS, lambda peer: tail_out, tail_in.at[pb_me])
            tail_in[pb_me] = energy
            finish(copies)
            energy = tail_in[0]
            for source in range(1, pb_size):
                energy = energy + tail_in[source]
            step_length = norm_now / (energy[0:1] + ridge_weight * length_now)
            fitted_ref[...] = fitted + step_length * direction
        else:
            image, energy = scattered_sum(
                "pb",
                2 + 2 * iteration,
                matmul(flipped[...], scale * updates),
                energy,
                pb_out.at[iteration + 1],
                pb_in.at[iteration + 1],
                pb_all.at[iteration + 1],
            )
            step_length = norm_now / (energy[0:1] + ridge_weight * length_now)
            fitted = fitted + step_length * direction
            residual = residual - step_length * (image + ridge_weight * direction)


def fit(part, kept_exponent):
    ka_size, pb_size = lax.axis_size("ka"), lax.axis_size("pb")
    query_rows, kept_rows = kept_exponent.shape
    width = part.shape[1] // 2
    ka_share, pb_share = query_rows // ka_size, kept_rows // pb_size
    space = functools.partial(pltpu.VMEM, dtype=jnp.float32)
    return pl.pallas_call(
        functools.partial(fit_kernel, ka_size, pb_size),
        out_shape=jax.ShapeDtypeStruct((kept_rows, width), jnp.float32),
        in_specs=[pl.BlockSpec(memory_space=pltpu.VMEM)] * 2,
        out_specs=pl.BlockSpec(memory_space=pltpu.VMEM),
        scratch_shapes=[
            space((kept_rows, query_rows)),
            space((ka_size, ka_share, 2 * width)),
            space((ka_size, ka_share, 2 * width)),
            space((ITERS, ka_size, ka_share + 8, width)),
            space((ITERS, ka_size, ka_share + 8, width)),
            space((ITERS, ka_size, ka_share, width)),
            space((ITERS, pb_size, pb_share + 8, width)),
            space((ITERS, pb_size, pb_share + 8, width)),
            space((ITERS, pb_size, pb_share, width)),
            space((8, width)),
            space((pb_size, 8, width)),
            pltpu.SemaphoreType.DMA((2 + 2 * ITERS, ka_size)),
            pltpu.SemaphoreType.DMA((2 + 2 * ITERS, ka_size)),
            pltpu.SemaphoreType.DMA((2 * ITERS + 1, pb_size)),
            pltpu.SemaphoreType.DMA((2 * ITERS + 1, pb_size)),
        ],
        compiler_params=pltpu.CompilerParams(
            collective_id=0, has_side_effects=True, vmem_limit_bytes=40 * 1024 * 1024
        ),
    )(part.reshape(ka_size, ka_share, 2 * width), kept_exponent)


def thirds(value):
    first = value.astype(jnp.bfloat16)
    rest = value - first.astype(jnp.float32)
    second = rest.astype(jnp.bfloat16)
    third = (rest - second.astype(jnp.float32)).astype(jnp.bfloat16)
    return first, second, third


def target_kernel(inverse_root, queries_ref, keys_ref, values_ref, kept_ref, part_ref, wide, top, total, sums):
    width = queries_ref.shape[1]

    @pl.when(pl.program_id(0) == 0)
    def _():
        one, two, three = thirds(queries_ref[...])
        wide[...] = jnp.concatenate((one, one, two, one, three, two), axis=1)
        top[...] = jnp.full_like(top, -jnp.inf)
        total[...] = jnp.zeros_like(total)
        sums[...] = jnp.zeros_like(sums)

    one, two, three = thirds(keys_ref[...])
    scores = (
        lax.dot_general(
            wide[...],
            jnp.concatenate((one, two, one, three, one, two), axis=1),
            (((1,), (1,)), ((), ())),
            preferred_element_type=jnp.float32,
        )
        * inverse_root
    )
    top_next = jnp.maximum(top[...], jnp.max(scores, axis=1, keepdims=True))
    factor = jnp.exp(top[...] - top_next)
    exponent = jnp.exp(scores - top_next)
    top[...] = top_next
    total[...] = total[...] * factor + jnp.sum(exponent, axis=1, keepdims=True)
    one, two, three = thirds(values_ref[...])
    high, middle, low = thirds(exponent)
    pair = jnp.concatenate((one, two), axis=1)
    product = functools.partial(jnp.dot, preferred_element_type=jnp.float32)
    both = product(high, pair) + product(middle, pair)
    small = product(high, three) + product(low, one)
    sums[...] = sums[...] * factor + (both[:, :width] + (both[:, width:] + small))

    @pl.when(pl.program_id(0) == pl.num_programs(0) - 1)
    def _():
        lane = lax.broadcasted_iota(jnp.int32, kept_ref.shape, 1)
        stats = jnp.where(lane == 0, top[...], jnp.where(lane == 1, total[...], kept_ref[...]))
        part_ref[:, :width] = sums[...]
        part_ref[:, width:] = stats


def target_part(queries, cache_keys, cache_values, kept_stats, inverse_root):
    query_rows, width = queries.shape
    block_size = min(2048, cache_keys.shape[0])
    fixed = pl.BlockSpec((query_rows, width), lambda block: (0, 0))
    moving = pl.BlockSpec((block_size, width), lambda block: (block, 0))
    return pl.pallas_call(
        functools.partial(target_kernel, inverse_root),
        grid=(cache_keys.shape[0] // block_size,),
        out_shape=jax.ShapeDtypeStruct((query_rows, 2 * width), jnp.float32),
        in_specs=[fixed, moving, moving, fixed],
        out_specs=pl.BlockSpec((query_rows, 2 * width), lambda block: (0, 0)),
        scratch_shapes=[
            pltpu.VMEM((query_rows, 6 * width), jnp.bfloat16),
            pltpu.VMEM((query_rows, 1), jnp.float32),
            pltpu.VMEM((query_rows, 1), jnp.float32),
            pltpu.VMEM((query_rows, width), jnp.float32),
        ],
        compiler_params=pltpu.CompilerParams(vmem_limit_bytes=40 * 1024 * 1024),
    )(queries, cache_keys, cache_values, kept_stats)


def halves(value):
    first = value.astype(jnp.bfloat16)
    return first, (value - first.astype(jnp.float32)).astype(jnp.bfloat16)


def product(left_side, right_side, left_dim=1, right_dim=0):
    return lax.dot_general(
        left_side,
        right_side,
        (((left_dim,), (right_dim,)), ((), ())),
        preferred_element_type=jnp.float32,
    )


def wide_queries(value):
    one, two, three = thirds(value)
    return jnp.concatenate((one, one, two, one, three, two), axis=1)


def wide_keys(value):
    one, two, three = thirds(value)
    return jnp.concatenate((one, two, one, three, one, two), axis=1)


def stacked(value):
    return jnp.concatenate(thirds(value), axis=0)


def folded(value):
    rows = value.shape[0] // 3
    return value[:rows] + (value[rows : 2 * rows] + value[2 * rows :])


def order_of(size):
    return list(range(1, size))


def whole_kernel(
    ka_size,
    pb_size,
    exponent_scale,
    index_ref,
    queries_hbm,
    keys_hbm,
    values_hbm,
    fitted_ref,
    keys_v,
    values_v,
    sums,
    queries_all,
    kept_all,
    part,
    part_in,
    stats,
    stats_in,
    first_part,
    second_part,
    first_turned,
    second_turned,
    kept_stats,
    scale,
    target_all,
    residual_v,
    half_out,
    core_in,
    side_out,
    side_in,
    updates_all,
    energy_out,
    energy_in,
    piece_out,
    piece_in,
    blocks_all,
    factor_place,
    factors,
    load_sems,
    ka_send,
    ka_recv,
    pb_send,
    pb_recv,
    pair_send,
    pair_recv,
):
    ka_me = lax.axis_index("ka")
    pb_me = lax.axis_index("pb")
    query_rows, width = queries_hbm.shape
    columns = width // ka_size
    pieces = query_rows // 128
    group = kept_all.shape[1]
    cache_rows = keys_hbm.shape[0]
    block = cache_rows // pb_size
    stride = block // group
    core_bit = lax.rem(pb_me, 2)
    core_peer = pb_me + 1 - 2 * core_bit
    side_peer = lax.rem(pb_me + 2, 4)

    def peer_of(axis, offset):
        if axis == "ka":
            return lax.rem(ka_me + offset, ka_size)
        return lax.rem(pb_me + offset, pb_size)

    barrier = pltpu.get_barrier_semaphore()
    for axis, size in (("ka", ka_size), ("pb", pb_size)):
        for offset in range(1, size):
            pl.semaphore_signal(
                barrier,
                inc=1,
                device_id={axis: peer_of(axis, offset)},
                device_id_type=pl.DeviceIdType.MESH,
            )

    def begin(axis, phase, source_of, target):
        size, send, recv = (
            (ka_size, ka_send, ka_recv) if axis == "ka" else (pb_size, pb_send, pb_recv)
        )
        copies = []
        for offset in order_of(size):
            peer = peer_of(axis, offset)
            copy = pltpu.make_async_remote_copy(
                src_ref=source_of(peer),
                dst_ref=target,
                send_sem=send.at[phase, offset],
                recv_sem=recv.at[phase, offset],
                device_id={axis: peer},
                device_id_type=pl.DeviceIdType.MESH,
            )
            copy.start()
            copies.append(copy)
        return copies

    def pair(phase, peer, source, target):
        copy = pltpu.make_async_remote_copy(
            src_ref=source,
            dst_ref=target,
            send_sem=pair_send.at[phase],
            recv_sem=pair_recv.at[phase],
            device_id={"pb": peer},
            device_id_type=pl.DeviceIdType.MESH,
        )
        copy.start()
        return copy

    def finish(copies):
        for copy in copies:
            copy.wait()

    def load(number, keys):
        source = pl.ds(pl.multiple_of(lax.rem(pb_me + number, pb_size) * block, block), block)
        hbm, vmem, kind = (keys_hbm, keys_v, 0) if keys else (values_hbm, values_v, 1)
        return pltpu.make_async_copy(
            hbm.at[source], vmem.at[number], load_sems.at[kind, number]
        )

    query_load = pltpu.make_async_copy(
        queries_hbm, queries_all.at[pb_me], load_sems.at[2, 0]
    )
    load(0, True).start()
    query_load.start()

    def pack(target, top, total):
        for piece in range(pieces):
            lanes = slice(piece * 128, (piece + 1) * 128)
            target[piece : piece + 1, :] = top[:, lanes]
            target[pieces + piece : pieces + piece + 1, :] = total[:, lanes]

    def unpack(value):
        return jnp.concatenate([value[piece : piece + 1] for piece in range(pieces)], axis=1)

    load(0, True).wait()
    for number in range(pb_size):
        if number > 0:
            load(number, True).start()
        load(number, False).start()
    place = index_ref[pl.ds(pb_me, 1), :] - (ka_me * cache_rows + pb_me * block)
    place = jnp.broadcast_to(place.astype(jnp.float32), (group, group)).T
    first_row = lax.broadcasted_iota(jnp.int32, (group, group), 0) * stride
    offset_row = place - first_row.astype(jnp.float32)
    kept = jnp.zeros((group, width), jnp.float32)
    for step in range(stride):
        kept = jnp.where(
            offset_row == float(step), keys_v[0, pl.ds(step, group, stride=stride), :], kept
        )
    kept_all[ka_me] = kept

    pl.semaphore_wait(barrier, ka_size + pb_size - 2)
    low_peer = ka_me + 1 - 2 * lax.rem(ka_me, 2)

    def kept_copy(offset, source, peer):
        return pltpu.make_async_remote_copy(
            src_ref=kept_all.at[source],
            dst_ref=kept_all.at[source],
            send_sem=ka_send.at[0, offset],
            recv_sem=ka_recv.at[0, offset],
            device_id={"ka": peer},
            device_id_type=pl.DeviceIdType.MESH,
        )

    far = [offset for offset in order_of(ka_size) if offset % 2 == 0]
    far_copies = [kept_copy(offset, ka_me, peer_of("ka", offset)) for offset in far]
    kept_copies = [kept_copy(1, ka_me, low_peer)]
    for copy in far_copies + kept_copies:
        copy.start()
    query_load.wait()
    query_copies = begin("pb", 0, lambda peer: queries_all.at[pb_me], queries_all.at[pb_me])

    own_wide = wide_queries(queries_all[pb_me] * exponent_scale)

    def target_block(number, carry):
        if carry is None:
            scores = product(wide_keys(keys_v[number]), own_wide, 1, 1)
            top_next = jnp.max(scores, axis=0, keepdims=True)
        else:
            load(number, True).wait()
            scores = product(wide_keys(keys_v[number]), own_wide, 1, 1)
            top, total = carry
            top_next = jnp.maximum(top, jnp.max(scores, axis=0, keepdims=True))
            factor = jnp.exp2(top - top_next)
        load(number, False).wait()
        high, low = halves(values_v[number].T)
        exponent = jnp.exp2(scores - top_next)
        block_total = jnp.sum(exponent, axis=0, keepdims=True)
        first, second = halves(exponent)
        both = product(jnp.concatenate((high, low), axis=0), first)
        added = both[:width] + (both[width:] + product(high, second))
        if carry is None:
            sums[...] = added
            return top_next, block_total
        sums[...] = sums[...] * factor + added
        return top_next, total * factor + block_total

    carry = lax.fori_loop(1, 2, target_block, target_block(0, None))
    for offset, copy in zip(far, far_copies):
        copy.wait()
        source = lax.rem(ka_me + ka_size - offset, ka_size)
        forwarded = kept_copy(offset + 1, source, low_peer)
        forwarded.start()
        kept_copies.append(forwarded)
    top, total = lax.fori_loop(2, pb_size, target_block, carry)
    part[...] = sums[...].reshape(ka_size, columns, query_rows)
    pack(stats, top, total)
    stats_copies = begin("ka", 2, lambda peer: stats, stats_in.at[ka_me])
    part_copies = begin("ka", 1, lambda peer: part.at[peer], part_in.at[ka_me])
    part_copies = list(zip(order_of(ka_size), part_copies))
    part_in[ka_me] = part[ka_me]
    stats_in[ka_me] = stats[...]

    finish(query_copies)
    finish(kept_copies)
    kept_wide = wide_keys(kept_all[...].reshape(ka_size * group, width))

    @pl.loop(0, pb_size, unroll=2)
    def _(number):
        scores = product(kept_wide, wide_queries(queries_all[number] * exponent_scale), 1, 1)
        top = jnp.max(scores, axis=0, keepdims=True)
        exponent = jnp.exp2(scores - top)
        pack(kept_stats.at[pb_me, number], top, jnp.sum(exponent, axis=0, keepdims=True))
        one, two = halves(exponent)
        first_part[number] = one
        second_part[number] = two
        first_turned[number] = one.T
        second_turned[number] = two.T

    kept_stats_copies = begin("pb", 1, lambda peer: kept_stats.at[pb_me], kept_stats.at[pb_me])

    finish(stats_copies)
    joint_top = stats_in[0, :pieces]
    for source in range(1, ka_size):
        joint_top = jnp.maximum(joint_top, stats_in[source, :pieces])
    joint_total = jnp.zeros_like(joint_top)
    for source in range(ka_size):
        joint_total = joint_total + stats_in[source, pieces:] * jnp.exp2(
            stats_in[source, :pieces] - joint_top
        )

    def weighted(source):
        return part_in[source] * unpack(jnp.exp2(stats_in[source, :pieces] - joint_top))

    numerator = weighted(ka_me)
    for offset, copy in part_copies:
        copy.wait()
        numerator = numerator + weighted(lax.rem(ka_me + ka_size - offset, ka_size))
    target_all[pb_me] = numerator / unpack(joint_total)
    target_copies = begin("pb", 2, lambda peer: target_all.at[pb_me], target_all.at[pb_me])

    finish(kept_stats_copies)
    for number in range(pb_size):
        joint_top = kept_stats[0, number, :pieces]
        for source in range(1, pb_size):
            joint_top = jnp.maximum(joint_top, kept_stats[source, number, :pieces])
        joint_total = jnp.zeros_like(joint_top)
        for source in range(pb_size):
            joint_total = joint_total + kept_stats[source, number, pieces:] * jnp.exp2(
                kept_stats[source, number, :pieces] - joint_top
            )
        own_top = kept_stats[pb_me, number, :pieces]
        scale[number] = jnp.broadcast_to(
            unpack(jnp.exp2(own_top - joint_top) / joint_total), (columns, query_rows)
        )

    def backward(number, vector):
        rows = stacked(scale[number] * vector)
        return product(rows, first_turned[number]) + product(rows, second_turned[number])

    lane = lax.broadcasted_iota(jnp.int32, (columns, 128), 1)

    def lane_sums(value):
        return jnp.sum(value, axis=1, keepdims=True)

    def long(number):
        return query_rows + 128 if number == 0 else query_rows

    def forward(phase, slot, vector, tail):
        rows = stacked(vector)

        def chunk_of(half, number):
            chunk = 2 * half + number
            term = folded(product(rows, first_part[chunk]) + product(rows, second_part[chunk]))
            half_out[slot, half, number, :, :query_rows] = scale[chunk] * term
            if number == 0:
                half_out[slot, half, number, :, query_rows:] = tail

        core_copies = []
        for number in range(2):
            chunk_of(1 - core_bit, number)
            lanes = pl.ds(0, long(number))
            core_copies.append(
                pair(
                    phase + number,
                    core_peer,
                    half_out.at[slot, 1 - core_bit, number, :, lanes],
                    core_in.at[slot, number, :, lanes],
                )
            )
        side_copies = []
        for number in range(2):
            chunk_of(core_bit, number)
            core_copies[number].wait()
            lanes = pl.ds(0, long(number))
            side_out[slot, number, :, lanes] = (
                half_out[slot, core_bit, number, :, lanes] + core_in[slot, number, :, lanes]
            )
            side_copies.append(
                pair(
                    phase + 2 + number,
                    side_peer,
                    side_out.at[slot, number, :, lanes],
                    side_in.at[slot, number, :, lanes],
                )
            )
        return side_copies

    def spread(phase, slot, value):
        for target in range(ka_size):
            piece_out[slot, target] = value[:, target * group : (target + 1) * group]
        piece_in[slot, ka_me] = piece_out[slot, ka_me]
        return begin(
            "ka", phase, lambda peer: piece_out.at[slot, peer], piece_in.at[slot, ka_me]
        )

    def share(phase, slot):
        blocks_all[slot, pb_me] = piece_in[slot].reshape(width, group)
        return begin(
            "pb", phase, lambda peer: blocks_all.at[slot, pb_me], blocks_all.at[slot, pb_me]
        )

    factor_place[...] = jnp.zeros_like(factor_place)
    image = backward(pb_me, target_all[pb_me])
    for offset, copy in sorted(
        zip(order_of(pb_size), target_copies), key=lambda item: item[0] % 2, reverse=True
    ):
        copy.wait()
        source = lax.rem(pb_me + pb_size - offset, pb_size)
        image = image + backward(source, target_all[source])
    residual = folded(image)
    residual_v[...] = residual
    side_copies = forward(
        0, 0, residual, jnp.where(lane == 0, lane_sums(residual * residual), 0.0)
    )
    spread_copies = spread(3, 0, residual)
    update_copies = []
    for number in range(2):
        side_copies[number].wait()
        joined = side_out[0, number, :, :query_rows] + side_in[0, number, :, :query_rows]
        updates_all[2 * core_bit + number] = joined
        update_copies.append(
            pair(
                4 + number,
                core_peer,
                updates_all.at[2 * core_bit + number],
                updates_all.at[2 * core_bit + number],
            )
        )
    norm_first = (side_out[0, 0, :, query_rows:] + side_in[0, 0, :, query_rows:])[:, :1]
    image = None
    energy = None
    for half in (core_bit, 1 - core_bit):
        for number in range(2):
            if half is not core_bit:
                update_copies[number].wait()
            updates = updates_all[2 * half + number]
            term = backward(2 * half + number, updates)
            image = term if image is None else image + term
            term = lane_sums(updates * updates)
            energy = term if energy is None else energy + term
        if half is core_bit:
            finish(spread_copies)
            first_copies = share(3, 0)
    step_first = norm_first / (energy + ridge_weight * norm_first)
    residual = residual_v[...]
    after = residual - step_first * (folded(image) + ridge_weight * residual)
    spread_copies = spread(4, 1, after)
    tail = jnp.where(
        lane == 0,
        lane_sums(after * after),
        jnp.where(lane == 1, lane_sums(after * residual), 0.0),
    )
    side_copies = forward(6, 1, after, tail)
    finish(side_copies)
    tail = side_out[1, 0, :, query_rows:] + side_in[1, 0, :, query_rows:]
    norm_second = tail[:, :1]
    ratio = norm_second / norm_first
    energy = None
    for number in range(2):
        updates = side_out[1, number, :, :query_rows] + side_in[1, number, :, :query_rows]
        updates = updates + ratio * updates_all[2 * core_bit + number]
        term = lane_sums(updates * updates)
        energy = term if energy is None else energy + term
    energy_out[...] = jnp.broadcast_to(energy, energy_out.shape)
    energy_copy = pair(10, core_peer, energy_out, energy_in)
    finish(spread_copies)
    second_copies = share(4, 1)
    energy_copy.wait()
    energy = energy_out[:, :1] + energy_in[:, :1]
    length = norm_second + 2.0 * ratio * tail[:, 1:2] + ratio * ratio * norm_first
    step_second = norm_second / (energy + ridge_weight * length)
    factor_place[pl.ds(pl.multiple_of(ka_me * columns, columns), columns), :] = jnp.where(
        lane == 0, step_first + step_second * ratio, step_second
    )
    factors[ka_me] = factor_place[...].T[:2]
    factor_copies = begin("ka", 5, lambda peer: factors.at[ka_me], factors.at[ka_me])
    finish(first_copies)
    finish(second_copies)
    turned = [[blocks_all[slot, number].T for number in range(pb_size)] for slot in range(2)]
    finish(factor_copies)
    both = factors[0]
    for source in range(1, ka_size):
        both = both + factors[source]
    for number in range(pb_size):
        fitted_ref[number * group : (number + 1) * group, :] = (
            both[0:1] * turned[0][number] + both[1:2] * turned[1][number]
        )


def whole(queries, cache_keys, cache_values, kept_index, exponent_scale):
    ka_size, pb_size = lax.axis_size("ka"), lax.axis_size("pb")
    query_rows, width = queries.shape
    kept_rows = kept_index.shape[0]
    cache_rows = cache_keys.shape[0]
    group, block, columns = kept_rows // pb_size, cache_rows // pb_size, width // ka_size
    pieces = query_rows // 128
    joint = ka_size * group
    space = functools.partial(pltpu.VMEM, dtype=jnp.float32)
    narrow = functools.partial(pltpu.VMEM, dtype=jnp.bfloat16)
    return pl.pallas_call(
        functools.partial(whole_kernel, ka_size, pb_size, exponent_scale),
        out_shape=jax.ShapeDtypeStruct((kept_rows, width), jnp.float32),
        in_specs=[pl.BlockSpec(memory_space=pltpu.VMEM)]
        + [pl.BlockSpec(memory_space=pl.ANY)] * 3,
        out_specs=pl.BlockSpec(memory_space=pltpu.VMEM),
        scratch_shapes=[
            space((pb_size, block, width)),
            space((pb_size, block, width)),
            space((width, query_rows)),
            space((pb_size, query_rows, width)),
            space((ka_size, group, width)),
            space((ka_size, columns, query_rows)),
            space((ka_size, columns, query_rows)),
            space((2 * pieces, 128)),
            space((ka_size, 2 * pieces, 128)),
            narrow((pb_size, joint, query_rows)),
            narrow((pb_size, joint, query_rows)),
            narrow((pb_size, query_rows, joint)),
            narrow((pb_size, query_rows, joint)),
            space((pb_size, pb_size, 2 * pieces, 128)),
            space((pb_size, columns, query_rows)),
            space((pb_size, columns, query_rows)),
            space((columns, joint)),
            space((2, 2, 2, columns, query_rows + 128)),
            space((2, 2, columns, query_rows + 128)),
            space((2, 2, columns, query_rows + 128)),
            space((2, 2, columns, query_rows + 128)),
            space((pb_size, columns, query_rows)),
            space((columns, 128)),
            space((columns, 128)),
            space((2, ka_size, columns, group)),
            space((2, ka_size, columns, group)),
            space((2, pb_size, width, group)),
            space((width, 128)),
            space((ka_size, 2, 128)),
            pltpu.SemaphoreType.DMA((3, pb_size)),
            pltpu.SemaphoreType.DMA((6, ka_size)),
            pltpu.SemaphoreType.DMA((6, ka_size)),
            pltpu.SemaphoreType.DMA((5, pb_size)),
            pltpu.SemaphoreType.DMA((5, pb_size)),
            pltpu.SemaphoreType.DMA((11,)),
            pltpu.SemaphoreType.DMA((11,)),
        ],
        compiler_params=pltpu.CompilerParams(
            collective_id=1, has_side_effects=True, vmem_limit_bytes=107 * 512 * 1024
        ),
    )(kept_index.reshape(pb_size, group), queries, cache_keys, cache_values)


def suits(ka_size, pb_size, queries, cache_keys, kept_index):
    width = queries.shape[1]
    group = kept_index.shape[0] // pb_size
    return (
        pb_size == 4
        and width == 128
        and group == 128
        and queries.shape[0] == 512
        and cache_keys.shape[0] == 8192
        and width % (8 * ka_size) == 0
    )


def shards(queries, cache_keys, cache_values, kept_index):
    head_width = queries.shape[1]
    inverse_root = 1.0 / math.sqrt(head_width)
    cache_rows = cache_keys.shape[0]
    if suits(lax.axis_size("ka"), lax.axis_size("pb"), queries, cache_keys, kept_index):
        exponent_scale = inverse_root * math.log2(math.e)
        return whole(queries, cache_keys, cache_values, kept_index, exponent_scale)

    local_kept = kept_index - lax.axis_index("ka") * cache_rows
    kept_keys = jnp.take(cache_keys, local_kept, axis=0)
    kept_scores = contract(queries, kept_keys, 1, 1) * inverse_root
    kept_top = jnp.max(kept_scores, axis=1)
    kept_exponent = jnp.exp(kept_scores - kept_top[:, None])
    kept_total = jnp.sum(kept_exponent, axis=1)

    zero = jnp.zeros_like(kept_top)
    stats = jnp.stack((zero, zero, kept_top, kept_total), axis=1)
    stats = jnp.pad(stats, ((0, 0), (0, head_width - 4)))
    return fit(
        target_part(queries, cache_keys, cache_values, stats, inverse_root), kept_exponent
    )


def solution(mesh):
    in_specs = (P("pb", None), P("ka", None), P("ka", None), P("ka"))
    out_specs = P("ka", None)
    return jax.shard_map(shards, mesh=mesh, in_specs=in_specs, out_specs=out_specs, check_vma=False)
```
